256 devices in a mesh: chan: 32 (over x, y, z_lo), win: 8 (over z_hi, core).
Axes of the slice: x: 4, y: 4, z: 8 (z_hi: 4, z_lo: 2; z = z_hi * 2 + z_lo), core: 2. Of those that a mesh axis runs over, the one named last changes fastest.
Arguments:
- records: float32 [32, 1024, 1024], P('win', 'chan'), may hold values from -180 to 180
- sources: int32 [32], replicated, may hold values from 0 to 1023, as said below
Outputs:
- correlations: float32 [32, 256, 1024], P('win', None, 'chan')
The draws below stay inside these ranges and needn't reach their ends.
Inputs may be any that keep to these rules, and one draw needn't show every extreme that they name: `sources`: source s is one of the channels s * 32 to (s + 1) * 32 - 1; the first source is channel 0 and the last is channel 1024 - 1.
All inputs are finite; a program needn't handle non-finite values.
Results may differ from the reference program's by a relative error of at most 0.00022.
Values sent between devices are 32-bit elements; how exact they have to be, the bound alone decides.
No kernel may reach another device: no remote copies, remote signals or barrier semaphores. Data moves between devices by JAX's collectives and lax.ppermute only.
A program may use at most 64 MiB of HBM per device.

```python
import math
import jax
import jax.numpy as jnp
from jax import lax

L = 1024
W = 32
C = 1024
NS = 32
LAGS = 256
HALF = 16
REACH = 32


def draw_records(key, part):
    subkeys = jax.random.split(key, 3)
    channel_gain = jnp.exp(jax.random.uniform(subkeys[0], (1, 1, C), minval=math.log(0.1), maxval=math.log(10.0)))
    segments = L // 16
    envelope = jnp.exp(jax.random.uniform(subkeys[1], (W, 16, C), minval=math.log(0.3), maxval=math.log(3.0)))
    envelope = jnp.repeat(envelope, segments, axis=1)
    random_part = jax.random.truncated_normal(subkeys[2], -6.0, 6.0, (W, L, C))
    return (channel_gain * envelope * random_part).astype(jnp.float32)


def draw_sources(key, part):
    spacing = C // NS
    offsets = jax.random.randint(key, (NS,), 0, spacing).astype(jnp.int32)
    offsets = offsets.at[0].set(0).at[NS - 1].set(spacing - 1)
    return (jnp.arange(NS, dtype=jnp.int32) * spacing + offsets).astype(jnp.int32)


def setup_inputs(seed: int = 0) -> dict:
    arg_keys = jax.random.split(jax.random.key(seed), 3)
    records = draw_records(jax.random.fold_in(arg_keys[2], 71), 0)
    sources = draw_sources(jax.random.fold_in(arg_keys[2], 71), 0)
    return {"records": records, "sources": sources}


HIGHEST = lax.Precision.HIGHEST
AMPLITUDE_FLOOR = 0.25
WHITE_EPSILON = 1e-06

def fourier_table(length):
    freq_count = length // 2
    freqs = jnp.arange(freq_count, dtype=jnp.int32)[:, None]
    sample_index = jnp.arange(length, dtype=jnp.int32)[None, :]
    angles = (freqs * sample_index % length).astype(jnp.float32) * (2.0 * math.pi / length)
    return jnp.concatenate([jnp.cos(angles), -jnp.sin(angles)], axis=0)

def band_table(freq_count, reach):
    rows_index = jnp.arange(freq_count, dtype=jnp.int32)[:, None]
    cols_index = jnp.arange(freq_count, dtype=jnp.int32)[None, :]
    return (jnp.abs(rows_index - cols_index) <= reach).astype(jnp.float32)

def inverse_table(length, lag_count, first_bin, bin_count, factor):
    freqs = first_bin + jnp.arange(bin_count, dtype=jnp.int32)
    lag_index = jnp.arange(lag_count, dtype=jnp.int32) - lag_count // 2
    angles = (lag_index[:, None] * freqs[None, :] % length).astype(jnp.float32) * (2.0 * math.pi / length)
    weights = jnp.where(freqs == 0, 1.0, 2.0).astype(jnp.float32)[None, :] * factor
    return jnp.concatenate([weights * jnp.cos(angles), -weights * jnp.sin(angles)], axis=1)

def reference(records, sources):
    freq_count = L // 2
    forward = fourier_table(L)
    band_matrix = band_table(freq_count, REACH)
    window_span = 2 * HALF + 1

    def one_window(window_data):
        chans = window_data.shape[1]
        padded = jnp.pad(jnp.abs(window_data), ((HALF, HALF), (0, 0)))
        running = jnp.concatenate([jnp.zeros((1, chans), jnp.float32), jnp.cumsum(padded, axis=0)], axis=0)
        amplitude = (running[window_span:] - running[:L]) / window_span
        normalized = window_data / jnp.maximum(amplitude, AMPLITUDE_FLOOR)
        spectrum = jnp.dot(forward, normalized, precision=HIGHEST)
        real_part = spectrum[:freq_count]
        imag_part = spectrum[freq_count:]
        magnitude = jnp.sqrt(real_part * real_part + imag_part * imag_part)
        smoothed = jnp.dot(band_matrix, magnitude, precision=HIGHEST) / (2 * REACH + 1) + WHITE_EPSILON
        return jnp.stack([real_part / smoothed, imag_part / smoothed])
    source_white = lax.map(one_window, records[:, :, sources])

    def accumulate(carry, pair):
        window_data, source_part = pair
        whitened = one_window(window_data)
        source_real = source_part[0][:, :, None]
        source_imag = source_part[1][:, :, None]
        white_real = whitened[0][:, None, :]
        white_imag = whitened[1][:, None, :]
        cross_real = carry[0] + source_real * white_real + source_imag * white_imag
        cross_imag = carry[1] + source_real * white_imag - source_imag * white_real
        return ((cross_real, cross_imag), None)
    chans = records.shape[2]
    zeros_init = jnp.zeros((freq_count, NS, chans), jnp.float32)
    (cross_real, cross_imag), _ = lax.scan(accumulate, (zeros_init, zeros_init), (records, source_white))
    factor = 1.0 / math.sqrt(W * freq_count)
    table = inverse_table(L, LAGS, 0, freq_count, factor).reshape(LAGS, 2, freq_count)
    stacked = jnp.stack([cross_real, cross_imag])
    return jnp.einsum('tak,aksc->stc', table, stacked, precision=HIGHEST)
```

```python
import functools
import math

import jax
import jax.numpy as jnp
import ml_dtypes
import numpy as np
from jax import lax
from jax.experimental import pallas as pl
from jax.experimental.pallas import tpu as pltpu
from jax.sharding import PartitionSpec as P

AMPLITUDE_FLOOR = 0.25
WHITE_EPSILON = 1e-06
HALF = 16
LANES = 128
F32 = jnp.float32
BF16 = jnp.bfloat16


def split_table(table):
    high = table.astype(np.float32).astype(ml_dtypes.bfloat16)
    low = (table - high.astype(np.float64)).astype(np.float32).astype(ml_dtypes.bfloat16)
    return high, low


def bin_order(freq_count):
    return np.concatenate([np.arange(0, freq_count, 2), np.arange(1, freq_count, 2)])


def forward_tables(length):
    freq_count = length // 2
    times = np.arange(length // 2)[:, None]
    parts = []
    for parity in range(2):
        bins = np.arange(parity, freq_count, 2)[None, :]
        angles = (bins * times % length) * (2.0 * math.pi / length)
        parts.append(np.concatenate([np.cos(angles), -np.sin(angles)], axis=1))
    return split_table(np.stack(parts))


def band_table(freq_count, reach):
    bins = bin_order(freq_count)
    return (np.abs(bins[:, None] - bins[None, :]) <= reach).astype(ml_dtypes.bfloat16)


def inverse_tables(length, lag_count, factor):
    freq_count = length // 2
    bins = bin_order(freq_count)
    lags = np.arange(lag_count) - lag_count // 2
    angles = (bins[:, None] * lags[None, :] % length) * (2.0 * math.pi / length)
    weights = np.where(bins == 0, 1.0, 2.0)[:, None] * factor
    return split_table(np.concatenate([weights * np.cos(angles), -weights * np.sin(angles)], axis=0))


def split(value):
    high = value.astype(BF16)
    return high, (value - high.astype(F32)).astype(BF16)


def mm(left, right):
    return jnp.dot(left, right, preferred_element_type=F32)


def pack_kernel(sources, records, packed):
    windows, times, channels = records.shape
    dests = packed.shape[0]
    width = channels // dests
    per_tile = LANES // width
    lane = lax.broadcasted_iota(jnp.int32, (times, LANES), 1)
    for tile in range(channels // LANES):
        loaded = [records[w, :, tile * LANES : (tile + 1) * LANES] for w in range(windows)]
        for e in range(per_tile):
            block = None
            for w in range(windows):
                shift = (w - e) * width % LANES
                moved = pltpu.roll(loaded[w], shift, 1) if shift else loaded[w]
                block = moved if block is None else jnp.where(lane >= w * width, moved, block)
            packed[tile * per_tile + e, 0:times, :] = block
    chosen = jnp.zeros((times, LANES), F32)
    for s in range(dests):
        tile = s * width // LANES
        place = sources[s] - tile * LANES
        for w in range(windows):
            target = w * dests + s
            shift = lax.rem(target + LANES - place, LANES)
            moved = pltpu.roll(records[w, :, tile * LANES : (tile + 1) * LANES], shift, 1)
            chosen = jnp.where(lane == target, moved, chosen)
    for d in range(dests):
        packed[d, times : 2 * times, :] = chosen


def main_kernel(
    place, blocks, fwd_high, fwd_low, band, inv_high, inv_low, send, keep,
    turned, white_re, white_im, cross_high, cross_low,
):
    devices, double, lanes = blocks.shape
    times = double // 2
    length = devices * times
    half = length // 2
    quarter = half // 2
    rows = 2 * lanes
    width = 32
    windows = lanes // width
    for part in range(2):
        data = blocks[:, part * times : (part + 1) * times, :].reshape(length, lanes)
        level = jnp.abs(data)
        edge = jnp.zeros((HALF, lanes), F32)
        tail = jnp.concatenate([level, edge], axis=0)
        total = jnp.concatenate([edge, level, edge], axis=0)
        size = length + 2 * HALF
        for step in (1, 2, 4, 8, 16):
            total = total + pltpu.roll(total, size - step, 0)
        amplitude = (total[:length] + tail[HALF:]) / (2 * HALF + 1)
        normal = data / jnp.maximum(amplitude, AMPLITUDE_FLOOR)
        turned[part * lanes : (part + 1) * lanes, :] = normal.T
    first = turned[:, :half]
    second = turned[:, half:]
    for parity in range(2):
        folded = first + second if parity == 0 else first - second
        high, low = split(folded)
        spectrum = (
            mm(high, fwd_high[parity]) + mm(low, fwd_high[parity]) + mm(high, fwd_low[parity])
        )
        white_re[:, parity * quarter : (parity + 1) * quarter] = spectrum[:, :quarter]
        white_im[:, parity * quarter : (parity + 1) * quarter] = spectrum[:, quarter:]
    re = white_re[...]
    im = white_im[...]
    high, low = split(jnp.sqrt(re * re + im * im))
    smooth = (mm(high, band[...]) + mm(low, band[...])) / (2 * (length // 32) + 1) + WHITE_EPSILON
    gain = 1.0 / smooth
    white_re[...] = re * gain
    white_im[...] = im * gain

    z_hi = place[0]
    core = place[1]
    for slot in range(4):
        target = lax.rem(z_hi + slot, 4)
        for which in range(2):
            turn = 4 * core if which else 4 - 4 * core
            turn = lax.rem(8 - turn, 8)
            for tile in range(half // LANES):
                span = slice(tile * LANES, (tile + 1) * LANES)
                chan_re = [white_re[w * width : (w + 1) * width, span] for w in range(windows)]
                chan_im = [white_im[w * width : (w + 1) * width, span] for w in range(windows)]
                rows8 = [
                    pl.ds(pl.multiple_of(lanes + w * width + target * 8, 8), 8)
                    for w in range(windows)
                ]
                from_re = [pltpu.roll(white_re[at, span], turn, 0) for at in rows8]
                from_im = [pltpu.roll(white_im[at, span], turn, 0) for at in rows8]
                for i in range(4):
                    out_re = None
                    for w in range(windows):
                        src_re = jnp.broadcast_to(from_re[w][i : i + 1], (width, LANES))
                        src_im = jnp.broadcast_to(from_im[w][i : i + 1], (width, LANES))
                        add_re = src_re * chan_re[w] + src_im * chan_im[w]
                        add_im = src_re * chan_im[w] - src_im * chan_re[w]
                        out_re = add_re if out_re is None else out_re + add_re
                        out_im = add_im if w == 0 else out_im + add_im
                    at = slice(i * width, (i + 1) * width)
                    cross_high[at, span], cross_low[at, span] = split(out_re)
                    span2 = slice(half + tile * LANES, half + (tile + 1) * LANES)
                    cross_high[at, span2], cross_low[at, span2] = split(out_im)
            result = (
                mm(cross_high[...], inv_high[...])
                + mm(cross_low[...], inv_high[...])
                + mm(cross_high[...], inv_low[...])
            )
            (keep if which else send)[slot] = result


def local(records, sources):
    chan_count = lax.axis_size("chan")
    windows, times, channels = records.shape
    length = times * chan_count
    lag_count = length // 4
    half = length // 2
    total_windows = windows * lax.axis_size("win")
    factor = 1.0 / math.sqrt(total_windows * half)
    vmem = pl.BlockSpec(memory_space=pltpu.VMEM)
    smem = pl.BlockSpec(memory_space=pltpu.SMEM)

    packed = pl.pallas_call(
        pack_kernel,
        out_shape=jax.ShapeDtypeStruct((chan_count, 2 * times, LANES), F32),
        in_specs=[smem, vmem],
        out_specs=vmem,
        name="pack",
    )(sources, records)
    blocks = lax.all_to_all(packed, "chan", 0, 0, tiled=True)

    fwd_high, fwd_low = (jnp.asarray(t) for t in forward_tables(length))
    inv_high, inv_low = (jnp.asarray(t) for t in inverse_tables(length, lag_count, factor))
    band = jnp.asarray(band_table(half, length // 32))
    win = lax.axis_index("win")
    place = jnp.stack([win // 2, win % 2]).astype(jnp.int32)
    part = jax.ShapeDtypeStruct((4, LANES, lag_count), F32)
    send, keep = pl.pallas_call(
        main_kernel,
        out_shape=(part, part),
        in_specs=[smem] + [vmem] * 6,
        out_specs=(vmem, vmem),
        scratch_shapes=[
            pltpu.VMEM((2 * LANES, length), F32),
            pltpu.VMEM((2 * LANES, half), F32),
            pltpu.VMEM((2 * LANES, half), F32),
            pltpu.VMEM((LANES, length), BF16),
            pltpu.VMEM((LANES, length), BF16),
        ],
        compiler_params=pltpu.CompilerParams(vmem_limit_bytes=48 << 20),
        name="stack",
    )(place, blocks, fwd_high, fwd_low, band, inv_high, inv_low)

    def shifted(value, shift):
        return lax.ppermute(value, "win", [(i, (i + shift) % 8) for i in range(8)])

    other = lax.ppermute(send, "win", [(i, i ^ 1) for i in range(8)])
    mid = LANES // 2
    pair = keep + other
    from_left = shifted(pair[2, :mid], 2)
    from_right = shifted(pair[2, mid:], -2)
    right = jnp.concatenate([pair[1, :mid] + from_left, pair[1, mid:]], axis=0)
    left = jnp.concatenate([pair[3, :mid], pair[3, mid:] + from_right], axis=0)
    result = pair[0] + shifted(right, 2) + shifted(left, -2)
    return jnp.transpose(result.reshape(4, 32, lag_count), (0, 2, 1))


def solution(mesh):
    placed = (P("win", "chan", None), P())
    return jax.shard_map(
        local, mesh=mesh, in_specs=placed, out_specs=P("win", None, "chan"), check_vma=False
    )
```

```python
import functools
import math

import jax
import jax.numpy as jnp
import ml_dtypes
import numpy as np
from jax import lax
from jax.experimental import pallas as pl
from jax.experimental.pallas import tpu as pltpu
from jax.sharding import PartitionSpec as P

AMPLITUDE_FLOOR = 0.25
WHITE_EPSILON = 1e-06
HALF = 16
LANES = 128
F32 = jnp.float32
BF16 = jnp.bfloat16


def split_table(table):
    high = table.astype(np.float32).astype(ml_dtypes.bfloat16)
    low = (table - high.astype(np.float64)).astype(np.float32).astype(ml_dtypes.bfloat16)
    return high, low


def bin_order(half):
    return np.concatenate([np.arange(0, half, 2), np.arange(1, half, 2)])


def forward_tables(length):
    half = length // 2
    times = np.arange(half)[:, None]
    tables = []
    for parity in range(2):
        bins = np.arange(parity, half, 2)[None, :]
        angles = (bins * times % length) * (2.0 * math.pi / length)
        tables += split_table(np.concatenate([np.cos(angles), -np.sin(angles)], axis=1))
    return np.stack(tables)


def band_tables(half, reach):
    bins = bin_order(half)
    table = (np.abs(bins[:, None] - bins[None, :]) <= reach).astype(ml_dtypes.bfloat16)
    mid = half // 2
    return np.stack([table[:mid, :mid], table[mid:, :mid], table[:mid, mid:]])


def inverse_tables(length, lag_count, factor):
    half = length // 2
    bins = bin_order(half)
    lags = np.arange(lag_count) - lag_count // 2
    angles = (bins[:, None] * lags[None, :] % length) * (2.0 * math.pi / length)
    weights = np.where(bins == 0, 1.0, 2.0)[:, None] * factor
    return np.stack(
        split_table(np.concatenate([weights * np.cos(angles), -weights * np.sin(angles)], axis=1))
    )


def split(value):
    high = value.astype(BF16)
    return high, (value - high.astype(F32)).astype(BF16)


def mm(left, right):
    return jnp.dot(left, right, preferred_element_type=F32)


def pack_kernel(sources, records, packed, taken, blocks, chosen, sems_in, sems_out):
    windows, times, channels = records.shape
    dests = packed.shape[0]
    width = channels // dests
    per_tile = LANES // width
    tiles = channels // LANES
    loads = []
    for tile in range(tiles):
        load = pltpu.make_async_copy(
            records.at[:, :, tile * LANES : (tile + 1) * LANES], taken.at[tile], sems_in.at[tile]
        )
        load.start()
        loads.append(load)
    stores = []
    lane = lax.broadcasted_iota(jnp.int32, (times, LANES), 1)
    pick = jnp.zeros((times, LANES), F32)
    for tile in range(tiles):
        loads[tile].wait()
        loaded = [taken[tile, w] for w in range(windows)]
        for e in range(per_tile):
            block = None
            for w in range(windows):
                shift = (w - e) * width % LANES
                moved = pltpu.roll(loaded[w], shift, 1) if shift else loaded[w]
                block = moved if block is None else jnp.where(lane >= w * width, moved, block)
            blocks[tile * per_tile + e] = block
        span = pl.ds(tile * per_tile, per_tile)
        store = pltpu.make_async_copy(
            blocks.at[span], packed.at[span, 0:times, :], sems_out.at[tile]
        )
        store.start()
        stores.append(store)
        for e in range(per_tile):
            s = tile * per_tile + e
            place = sources[s] - tile * LANES
            for w in range(windows):
                target = w * dests + s
                shift = lax.rem(target + LANES - place, LANES)
                pick = jnp.where(lane == target, pltpu.roll(loaded[w], shift, 1), pick)
    for d in range(dests):
        chosen[d] = pick
    store = pltpu.make_async_copy(chosen, packed.at[:, times : 2 * times, :], sems_out.at[tiles])
    store.start()
    stores.append(store)
    for store in stores:
        store.wait()


def position():
    win = lax.axis_index("win")
    return lax.div(win, 2), lax.rem(win, 2)


def correlate(white_re, white_im, cross_high, cross_low, target, which, core, width):
    rows, half = white_re.shape
    lanes = rows // 2
    windows = lanes // width
    turn = lax.rem(8 - (4 * core if which else 4 - 4 * core), 8)
    rows8 = [
        pl.ds(pl.multiple_of(lanes + w * width + target * 8, 8), 8) for w in range(windows)
    ]
    for tile in range(half // LANES):
        span = slice(tile * LANES, (tile + 1) * LANES)
        span2 = slice(half + tile * LANES, half + (tile + 1) * LANES)
        chan_re = [white_re[w * width : (w + 1) * width, span] for w in range(windows)]
        chan_im = [white_im[w * width : (w + 1) * width, span] for w in range(windows)]
        from_re = [pltpu.roll(white_re[at, span], turn, 0) for at in rows8]
        from_im = [pltpu.roll(white_im[at, span], turn, 0) for at in rows8]
        for i in range(4):
            out_re = None
            for w in range(windows):
                src_re = jnp.broadcast_to(from_re[w][i : i + 1], (width, LANES))
                src_im = jnp.broadcast_to(from_im[w][i : i + 1], (width, LANES))
                add_re = src_re * chan_re[w] + src_im * chan_im[w]
                add_im = src_re * chan_im[w] - src_im * chan_re[w]
                out_re = add_re if w == 0 else out_re + add_re
                out_im = add_im if w == 0 else out_im + add_im
            at = slice(i * width, (i + 1) * width)
            cross_high[at, span], cross_low[at, span] = split(out_re)
            cross_high[at, span2], cross_low[at, span2] = split(out_im)


def invert(cross_high, cross_low, tables):
    half = cross_high.shape[1] // 2
    lags = half // 2
    total = None
    for part in range(2):
        high = cross_high[:, part * half : (part + 1) * half]
        low = cross_low[:, part * half : (part + 1) * half]
        wave = tables[0, :, part * lags : (part + 1) * lags]
        rest = tables[1, :, part * lags : (part + 1) * lags]
        term = mm(high, wave) + mm(low, wave) + mm(high, rest)
        total = term if part == 0 else total + term
    return total


def front_kernel(
    blocks, tables, band, white_re, white_im, turned
):
    devices, double, lanes = blocks.shape
    times = double // 2
    length = devices * times
    half = length // 2
    quarter = half // 2
    for part in range(2):
        data = blocks[:, part * times : (part + 1) * times, :].reshape(length, lanes)
        level = jnp.abs(data)
        edge = jnp.zeros((HALF, lanes), F32)
        tail = jnp.concatenate([level, edge], axis=0)
        total = jnp.concatenate([edge, level, edge], axis=0)
        size = length + 2 * HALF
        for step in (1, 2, 4, 8, 16):
            total = total + pltpu.roll(total, size - step, 0)
        amplitude = (total[:length] + tail[HALF:]) / (2 * HALF + 1)
        normal = data / jnp.maximum(amplitude, AMPLITUDE_FLOOR)
        turned[part * lanes : (part + 1) * lanes, :] = normal.T
    first = turned[:, :half]
    second = turned[:, half:]
    for parity in range(2):
        folded = first + second if parity == 0 else first - second
        high, low = split(folded)
        spectrum = (
            mm(high, tables[2 * parity])
            + mm(low, tables[2 * parity])
            + mm(high, tables[2 * parity + 1])
        )
        white_re[:, parity * quarter : (parity + 1) * quarter] = spectrum[:, :quarter]
        white_im[:, parity * quarter : (parity + 1) * quarter] = spectrum[:, quarter:]
    re = white_re[...]
    im = white_im[...]
    high, low = split(jnp.sqrt(re * re + im * im))
    for parity in range(2):
        near = slice(parity * quarter, (parity + 1) * quarter)
        other = slice((1 - parity) * quarter, (2 - parity) * quarter)
        smooth = (
            mm(high[:, near], band[0])
            + mm(low[:, near], band[0])
            + mm(high[:, other], band[1 + parity])
            + mm(low[:, other], band[1 + parity])
        )
        gain = 1.0 / (smooth / (2 * (length // 32) + 1) + WHITE_EPSILON)
        white_re[:, near] = re[:, near] * gain
        white_im[:, near] = im[:, near] * gain


def stack_kernel(slots, white_re, white_im, tables, *refs):
    send, keep, cross_high, cross_low = refs[-4:]
    z_hi, core = position()
    for n, slot in enumerate(slots):
        target = lax.rem(z_hi + slot, 4)
        for which in range(2):
            correlate(white_re, white_im, cross_high, cross_low, target, which, core, 32)
            (keep if which else send)[n] = invert(cross_high, cross_low, tables)


def local(records, sources):
    chan_count = lax.axis_size("chan")
    windows, times, channels = records.shape
    length = times * chan_count
    lag_count = length // 4
    half = length // 2
    total_windows = windows * lax.axis_size("win")
    factor = 1.0 / math.sqrt(total_windows * half)
    vmem = pl.BlockSpec(memory_space=pltpu.VMEM)
    smem = pl.BlockSpec(memory_space=pltpu.SMEM)
    hbm = pl.BlockSpec(memory_space=pltpu.HBM)
    tiles = channels // LANES

    packed = pl.pallas_call(
        pack_kernel,
        out_shape=jax.ShapeDtypeStruct((chan_count, 2 * times, LANES), F32),
        in_specs=[smem, hbm],
        out_specs=hbm,
        scratch_shapes=[
            pltpu.VMEM((tiles, windows, times, LANES), F32),
            pltpu.VMEM((chan_count, times, LANES), F32),
            pltpu.VMEM((chan_count, times, LANES), F32),
            pltpu.SemaphoreType.DMA((tiles,)),
            pltpu.SemaphoreType.DMA((tiles + 1,)),
        ],
        name="pack",
    )(sources, records)
    blocks = lax.all_to_all(packed, "chan", 0, 0, tiled=True)

    forward = jnp.asarray(forward_tables(length))
    band = jnp.asarray(band_tables(half, length // 32))
    inverse = jnp.asarray(inverse_tables(length, lag_count, factor))
    rows = 2 * LANES
    shape = jax.ShapeDtypeStruct
    white_re, white_im = pl.pallas_call(
        front_kernel,
        out_shape=(shape((rows, half), F32), shape((rows, half), F32)),
        in_specs=[vmem] * 3,
        out_specs=(vmem, vmem),
        scratch_shapes=[pltpu.VMEM((rows, length), F32)],
        compiler_params=pltpu.CompilerParams(vmem_limit_bytes=24 << 20),
        cost_estimate=pl.CostEstimate(flops=2 << 30, bytes_accessed=10 << 20, transcendentals=0),
        name="front",
    )(blocks, forward, band)

    def stack(slots, after=None, handed=None):
        part = shape((len(slots), LANES, lag_count), F32)
        extra = [] if after is None else [after]
        outs = [part, part]
        aliases = {}
        if handed is not None:
            aliases = {3 + len(extra): 0}
            extra.append(handed)
            outs.insert(0, shape(handed.shape, F32))
        return pl.pallas_call(
            functools.partial(stack_kernel, slots),
            out_shape=outs,
            in_specs=[vmem] * (3 + len(extra)),
            out_specs=[vmem] * len(outs),
            scratch_shapes=[pltpu.VMEM((LANES, length), BF16), pltpu.VMEM((LANES, length), BF16)],
            input_output_aliases=aliases,
            compiler_params=pltpu.CompilerParams(vmem_limit_bytes=16 << 20),
            cost_estimate=pl.CostEstimate(
                flops=len(slots) << 30, bytes_accessed=len(slots) << 22, transcendentals=0
            ),
            name="stack",
        )(white_re, white_im, inverse, *extra)

    def shifted(value, shift):
        return lax.ppermute(value, "win", [(i, (i + shift) % 8) for i in range(8)])

    def across(value):
        return lax.ppermute(value, "win", [(i, i ^ 1) for i in range(8)])

    mid = LANES // 2
    send_far, keep_far = stack((2,))
    keep_far, send_right, keep_right = stack((1,), handed=keep_far)
    far = keep_far[0] + across(send_far)[0]
    from_left = shifted(far[:mid], 2)
    from_right = shifted(far[mid:], -2)
    keep_right, send, keep = stack((3, 0), after=far, handed=keep_right)
    pair = keep + across(send)
    right = keep_right[0] + across(send_right)[0]
    right = jnp.concatenate([right[:mid] + from_left, right[mid:]], axis=0)
    left = jnp.concatenate([pair[0, :mid], pair[0, mid:] + from_right], axis=0)
    result = pair[1] + shifted(right, 2) + shifted(left, -2)
    return jnp.transpose(result.reshape(4, 32, lag_count), (0, 2, 1))


def solution(mesh):
    placed = (P("win", "chan", None), P())
    return jax.shard_map(
        local, mesh=mesh, in_specs=placed, out_specs=P("win", None, "chan"), check_vma=False
    )
```

```python
import functools
import math

import jax
import jax.numpy as jnp
import ml_dtypes
import numpy as np
from jax import lax
from jax.experimental import pallas as pl
from jax.experimental.pallas import tpu as pltpu
from jax.sharding import PartitionSpec as P

AMPLITUDE_FLOOR = 0.25
WHITE_EPSILON = 1e-06
HALF = 16
LANES = 128
F32 = jnp.float32
BF16 = jnp.bfloat16


def split_table(table):
    high = table.astype(np.float32).astype(ml_dtypes.bfloat16)
    low = (table - high.astype(np.float64)).astype(np.float32).astype(ml_dtypes.bfloat16)
    return high, low


def bin_order(half):
    return np.concatenate([np.arange(0, half, 2), np.arange(1, half, 2)])


def forward_tables(length):
    half = length // 2
    times = np.arange(half)[:, None]
    tables = []
    for parity in range(2):
        bins = np.arange(parity, half, 2)[None, :]
        angles = (bins * times % length) * (2.0 * math.pi / length)
        tables += split_table(np.concatenate([np.cos(angles), -np.sin(angles)], axis=1))
    return np.stack(tables)


def front_tables(length, reach):
    half = length // 2
    mid = half // 2
    bins = bin_order(half)
    table = (np.abs(bins[:, None] - bins[None, :]) <= reach).astype(ml_dtypes.bfloat16)
    band = np.concatenate([table[:mid, :mid], table[mid:, :mid]], axis=1)
    return np.concatenate([*forward_tables(length), band], axis=0)


def inverse_tables(length, lag_count, factor):
    half = length // 2
    bins = bin_order(half)
    lags = np.arange(lag_count) - lag_count // 2
    angles = (bins[:, None] * lags[None, :] % length) * (2.0 * math.pi / length)
    weights = np.where(bins == 0, 1.0, 2.0)[:, None] * factor
    return np.stack(
        split_table(np.concatenate([weights * np.cos(angles), -weights * np.sin(angles)], axis=1))
    )


def split(value):
    high = value.astype(BF16)
    return high, (value - high.astype(F32)).astype(BF16)


def mm(left, right):
    return jnp.dot(left, right, preferred_element_type=F32)


def mm_turned(left, right):
    return lax.dot_general(left, right, (((1,), (1,)), ((), ())), preferred_element_type=F32)


def pack_kernel(sources, records, packed, taken, blocks, chosen, sems_in, sems_out):
    windows, times, channels = records.shape
    dests = packed.shape[0]
    width = channels // dests
    per_tile = LANES // width
    tiles = channels // LANES
    loads = []
    for tile in range(tiles):
        load = pltpu.make_async_copy(
            records.at[:, :, tile * LANES : (tile + 1) * LANES], taken.at[tile], sems_in.at[tile]
        )
        load.start()
        loads.append(load)
    stores = []
    lane = lax.broadcasted_iota(jnp.int32, (times, LANES), 1)
    pick = jnp.zeros((times, LANES), F32)
    column = lax.rem(lane, dests)
    place = jnp.zeros((times, LANES), jnp.int32)
    for s in range(dests):
        place = jnp.where(column == s, sources[s] - s * width // LANES * LANES, place)
    for tile in range(tiles):
        loads[tile].wait()
        loaded = [taken[tile, w] for w in range(windows)]
        for e in range(per_tile):
            block = None
            for w in range(windows):
                shift = (w - e) * width % LANES
                moved = pltpu.roll(loaded[w], shift, 1) if shift else loaded[w]
                block = moved if block is None else jnp.where(lane >= w * width, moved, block)
            blocks[tile * per_tile + e] = block
        span = pl.ds(tile * per_tile, per_tile)
        store = pltpu.make_async_copy(
            blocks.at[span], packed.at[span, 0:times, :], sems_out.at[tile]
        )
        store.start()
        stores.append(store)
        for w in range(windows):
            moved = jnp.take_along_axis(loaded[w], place, axis=1)
            low = w * dests + tile * per_tile
            pick = jnp.where((lane >= low) & (lane < low + per_tile), moved, pick)
    for d in range(dests):
        chosen[d] = pick
    store = pltpu.make_async_copy(chosen, packed.at[:, times : 2 * times, :], sems_out.at[tiles])
    store.start()
    stores.append(store)
    for store in stores:
        store.wait()


def correlate(white_re, white_im, cross_high, cross_low, target, width):
    rows, half = white_re.shape
    lanes = rows // 2
    windows = lanes // width
    rows8 = [
        pl.ds(pl.multiple_of(lanes + w * width + target * 8, 8), 8) for w in range(windows)
    ]
    for tile in range(half // LANES):
        span = slice(tile * LANES, (tile + 1) * LANES)
        span2 = slice(half + tile * LANES, half + (tile + 1) * LANES)
        chan_re = [white_re[w * width : (w + 1) * width, span] for w in range(windows)]
        chan_im = [white_im[w * width : (w + 1) * width, span] for w in range(windows)]
        from_re = [white_re[at, span] for at in rows8]
        from_im = [white_im[at, span] for at in rows8]
        for i in range(8):
            for w in range(windows):
                src_re = jnp.broadcast_to(from_re[w][i : i + 1], (width, LANES))
                src_im = jnp.broadcast_to(from_im[w][i : i + 1], (width, LANES))
                add_re = src_re * chan_re[w] + src_im * chan_im[w]
                add_im = src_re * chan_im[w] - src_im * chan_re[w]
                out_re = add_re if w == 0 else out_re + add_re
                out_im = add_im if w == 0 else out_im + add_im
            at = slice(i * width, (i + 1) * width)
            cross_high[at, span], cross_low[at, span] = split(out_re)
            cross_high[at, span2], cross_low[at, span2] = split(out_im)


def invert(cross_high, cross_low, tables):
    half = cross_high.shape[1] // 2
    lags = half // 2
    total = None
    for part in range(2):
        high = cross_high[:, part * half : (part + 1) * half]
        low = cross_low[:, part * half : (part + 1) * half]
        wave = tables[0, :, part * lags : (part + 1) * lags]
        rest = tables[1, :, part * lags : (part + 1) * lags]
        term = mm(high, wave) + mm(low, wave) + mm(high, rest)
        total = term if part == 0 else total + term
    return total


def front_kernel(
    blocks, tables, white_re, white_im, turned
):
    devices, double, lanes = blocks.shape
    times = double // 2
    length = devices * times
    half = length // 2
    quarter = half // 2
    for part in range(2):
        data = blocks[:, part * times : (part + 1) * times, :].reshape(length, lanes)
        level = jnp.abs(data)
        edge = jnp.zeros((HALF, lanes), F32)
        tail = jnp.concatenate([level, edge], axis=0)
        total = jnp.concatenate([edge, level, edge], axis=0)
        size = length + 2 * HALF
        for step in (1, 2, 4, 8, 16):
            total = total + pltpu.roll(total, size - step, 0)
        amplitude = (total[:length] + tail[HALF:]) / (2 * HALF + 1)
        normal = data / jnp.maximum(amplitude, AMPLITUDE_FLOOR)
        turned[part * lanes : (part + 1) * lanes, :] = normal.T
    waves = [tables[n * half : (n + 1) * half, :] for n in range(4)]
    band = [tables[4 * half :, :quarter], tables[4 * half :, quarter:]]
    first = turned[:, :half]
    second = turned[:, half:]
    for parity in range(2):
        folded = first + second if parity == 0 else first - second
        high, low = split(folded)
        spectrum = (
            mm(high, waves[2 * parity])
            + mm(low, waves[2 * parity])
            + mm(high, waves[2 * parity + 1])
        )
        white_re[:, parity * quarter : (parity + 1) * quarter] = spectrum[:, :quarter]
        white_im[:, parity * quarter : (parity + 1) * quarter] = spectrum[:, quarter:]
    re = white_re[...]
    im = white_im[...]
    high, low = split(jnp.sqrt(re * re + im * im))
    for parity in range(2):
        near = slice(parity * quarter, (parity + 1) * quarter)
        other = slice((1 - parity) * quarter, (2 - parity) * quarter)
        cross_mm = mm_turned if parity else mm
        smooth = (
            mm(high[:, near], band[0])
            + mm(low[:, near], band[0])
            + cross_mm(high[:, other], band[1])
            + cross_mm(low[:, other], band[1])
        )
        gain = 1.0 / (smooth / (2 * (length // 32) + 1) + WHITE_EPSILON)
        white_re[:, near] = re[:, near] * gain
        white_im[:, near] = im[:, near] * gain


def stack_kernel(slots, white_re, white_im, tables, *refs):
    send, keep, cross_high, cross_low, both = refs[-5:]
    win = lax.axis_index("win")
    z_hi, core = lax.div(win, 2), lax.rem(win, 2)
    for n, slot in enumerate(slots):
        target = lax.rem(z_hi + slot, 4)
        correlate(white_re, white_im, cross_high.at[n], cross_low.at[n], target, 32)
        result = invert(cross_high.at[n], cross_low.at[n], tables)
        both[n] = result.reshape(both.shape[1:])
    for n in range(len(slots)):
        keep[n] = both[n, core]
        send[n] = both[n, 1 - core]


def join_kernel(keep_right, other_right, keep_left, other_left, right, left):
    right[...] = keep_right[0] + other_right[0]
    left[...] = keep_left[0] + other_left[0]


def local(records, sources):
    chan_count = lax.axis_size("chan")
    windows, times, channels = records.shape
    length = times * chan_count
    lag_count = length // 4
    half = length // 2
    total_windows = windows * lax.axis_size("win")
    factor = 1.0 / math.sqrt(total_windows * half)
    vmem = pl.BlockSpec(memory_space=pltpu.VMEM)
    smem = pl.BlockSpec(memory_space=pltpu.SMEM)
    hbm = pl.BlockSpec(memory_space=pltpu.HBM)
    tiles = channels // LANES

    packed = pl.pallas_call(
        pack_kernel,
        out_shape=jax.ShapeDtypeStruct((chan_count, 2 * times, LANES), F32),
        in_specs=[smem, hbm],
        out_specs=hbm,
        scratch_shapes=[
            pltpu.VMEM((tiles, windows, times, LANES), F32),
            pltpu.VMEM((chan_count, times, LANES), F32),
            pltpu.VMEM((chan_count, times, LANES), F32),
            pltpu.SemaphoreType.DMA((tiles,)),
            pltpu.SemaphoreType.DMA((tiles + 1,)),
        ],
        compiler_params=pltpu.CompilerParams(vmem_limit_bytes=60 << 20),
        name="pack",
    )(sources, records)
    blocks = lax.all_to_all(packed, "chan", 0, 0, tiled=True)

    forward = jnp.asarray(front_tables(length, length // 32))
    inverse = jnp.asarray(inverse_tables(length, lag_count, factor))
    rows = 2 * LANES
    shape = jax.ShapeDtypeStruct
    white_re, white_im = pl.pallas_call(
        front_kernel,
        out_shape=(shape((rows, half), F32), shape((rows, half), F32)),
        in_specs=[vmem] * 2,
        out_specs=(vmem, vmem),
        scratch_shapes=[pltpu.VMEM((rows, length), F32)],
        compiler_params=pltpu.CompilerParams(vmem_limit_bytes=24 << 20),
        name="front",
    )(blocks, forward)

    def stack(slots, after=None, handed=None):
        part = shape((len(slots), LANES, lag_count), F32)
        extra = [] if after is None else [after]
        outs = [part, part]
        aliases = {}
        if handed is not None:
            aliases = {3 + len(extra): 0}
            extra.append(handed)
            outs.insert(0, shape(handed.shape, F32))
        return pl.pallas_call(
            functools.partial(stack_kernel, slots),
            out_shape=outs,
            in_specs=[vmem] * (3 + len(extra)),
            out_specs=[vmem] * len(outs),
            scratch_shapes=[
                pltpu.VMEM((len(slots), 2 * LANES, length), BF16),
                pltpu.VMEM((len(slots), 2 * LANES, length), BF16),
                pltpu.VMEM((len(slots), 2, LANES, lag_count), F32),
            ],
            input_output_aliases=aliases,
            compiler_params=pltpu.CompilerParams(vmem_limit_bytes=16 << 20),
            cost_estimate=pl.CostEstimate(flops=1, bytes_accessed=1, transcendentals=0),
            name="stack",
        )(white_re, white_im, inverse, *extra)

    def shifted(value, shift):
        return lax.ppermute(value, "win", [(i, (i + shift) % 8) for i in range(8)])

    def across(value):
        return lax.ppermute(value, "win", [(i, i ^ 1) for i in range(8)])

    send_far, keep_far = stack((2,))
    keep_far, send_right, keep_right = stack((1,), handed=keep_far)
    far = keep_far[0] + across(send_far)[0]
    from_far = shifted(far, 4)
    send_left, keep_left = stack((3,), after=far)
    keep_left, send, keep = stack((0,), handed=keep_left)
    right, left = pl.pallas_call(
        join_kernel,
        out_shape=[shape((LANES, lag_count), F32)] * 2,
        in_specs=[vmem] * 4,
        out_specs=[vmem] * 2,
        compiler_params=pltpu.CompilerParams(vmem_limit_bytes=4 << 20),
        name="join",
    )(keep_right, across(send_right), keep_left, across(send_left))
    from_left = shifted(right, 2)
    from_right = shifted(left, -2)
    result = (keep[0] + across(send)[0] + from_far) + (from_left + from_right)
    return jnp.transpose(result.reshape(4, 32, lag_count), (0, 2, 1))


def solution(mesh):
    placed = (P("win", "chan", None), P())
    return jax.shard_map(
        local, mesh=mesh, in_specs=placed, out_specs=P("win", None, "chan"), check_vma=False
    )
```

```python
import functools
import math

import jax
import jax.numpy as jnp
import ml_dtypes
import numpy as np
from jax import lax
from jax.experimental import pallas as pl
from jax.experimental.pallas import tpu as pltpu
from jax.sharding import PartitionSpec as P

AMPLITUDE_FLOOR = 0.25
WHITE_EPSILON = 1e-06
HALF = 16
LANES = 128
F32 = jnp.float32
BF16 = jnp.bfloat16


def split_table(table):
    high = table.astype(np.float32).astype(ml_dtypes.bfloat16)
    low = (table - high.astype(np.float64)).astype(np.float32).astype(ml_dtypes.bfloat16)
    return high, low


def bin_order(half):
    return np.concatenate([np.arange(0, half, 2), np.arange(1, half, 2)])


def forward_tables(length):
    half = length // 2
    times = np.arange(half)[:, None]
    tables = []
    for parity in range(2):
        bins = np.arange(parity, half, 2)[None, :]
        angles = (bins * times % length) * (2.0 * math.pi / length)
        tables += split_table(np.concatenate([np.cos(angles), -np.sin(angles)], axis=1))
    return np.stack(tables)


def front_tables(length, reach):
    half = length // 2
    mid = half // 2
    bins = bin_order(half)
    table = (np.abs(bins[:, None] - bins[None, :]) <= reach).astype(ml_dtypes.bfloat16)
    band = np.concatenate([table[:mid, :mid], table[mid:, :mid]], axis=1)
    return np.concatenate([*forward_tables(length), band], axis=0)


def inverse_tables(length, lag_count, factor):
    half = length // 2
    bins = bin_order(half)
    lags = np.arange(lag_count) - lag_count // 2
    angles = (bins[:, None] * lags[None, :] % length) * (2.0 * math.pi / length)
    weights = np.where(bins == 0, 1.0, 2.0)[:, None] * factor
    return np.stack(
        split_table(np.concatenate([weights * np.cos(angles), -weights * np.sin(angles)], axis=1))
    )


def split(value):
    high = value.astype(BF16)
    return high, (value - high.astype(F32)).astype(BF16)


def mm(left, right):
    return jnp.dot(left, right, preferred_element_type=F32)


def mm_turned(left, right):
    return lax.dot_general(left, right, (((1,), (1,)), ((), ())), preferred_element_type=F32)


def pack_kernel(sources, records, packed):
    windows, times, channels = records.shape
    dests = packed.shape[0]
    width = channels // dests
    per_tile = LANES // width
    lane = lax.broadcasted_iota(jnp.int32, (times, LANES), 1)
    column = lax.rem(lane, dests)
    place = jnp.zeros((times, LANES), jnp.int32)
    for s in range(dests):
        place = jnp.where(column == s, sources[s] - s * width // LANES * LANES, place)
    pick = jnp.zeros((times, LANES), F32)
    for tile in range(channels // LANES):
        loaded = [records[w, :, tile * LANES : (tile + 1) * LANES] for w in range(windows)]
        for e in range(per_tile):
            block = None
            for w in range(windows):
                shift = (w - e) * width % LANES
                moved = pltpu.roll(loaded[w], shift, 1) if shift else loaded[w]
                block = moved if block is None else jnp.where(lane >= w * width, moved, block)
            packed[tile * per_tile + e, 0:times, :] = block
        for w in range(windows):
            moved = jnp.take_along_axis(loaded[w], place, axis=1)
            low = w * dests + tile * per_tile
            pick = jnp.where((lane >= low) & (lane < low + per_tile), moved, pick)
    for d in range(dests):
        packed[d, times : 2 * times, :] = pick


def correlate(white_re, white_im, cross_high, cross_low, target, width):
    rows, half = white_re.shape
    lanes = rows // 2
    windows = lanes // width
    rows8 = [
        pl.ds(pl.multiple_of(lanes + w * width + target * 8, 8), 8) for w in range(windows)
    ]
    for tile in range(half // LANES):
        span = slice(tile * LANES, (tile + 1) * LANES)
        span2 = slice(half + tile * LANES, half + (tile + 1) * LANES)
        chan_re = [white_re[w * width : (w + 1) * width, span] for w in range(windows)]
        chan_im = [white_im[w * width : (w + 1) * width, span] for w in range(windows)]
        from_re = [white_re[at, span] for at in rows8]
        from_im = [white_im[at, span] for at in rows8]
        chan_sum = [a + b for a, b in zip(chan_re, chan_im)]
        from_sum = [a + b for a, b in zip(from_re, from_im)]
        from_less = [a - b for a, b in zip(from_re, from_im)]
        for i in range(8):
            for w in range(windows):
                one = jnp.broadcast_to(from_re[w][i : i + 1], (width, LANES)) * chan_sum[w]
                two = jnp.broadcast_to(from_less[w][i : i + 1], (width, LANES)) * chan_im[w]
                three = jnp.broadcast_to(from_sum[w][i : i + 1], (width, LANES)) * chan_re[w]
                ones = one if w == 0 else ones + one
                twos = two if w == 0 else twos + two
                threes = three if w == 0 else threes + three
            at = slice(i * width, (i + 1) * width)
            cross_high[at, span], cross_low[at, span] = split(ones - twos)
            cross_high[at, span2], cross_low[at, span2] = split(ones - threes)


def invert(cross_high, cross_low, tables):
    half = cross_high.shape[1] // 2
    lags = half // 2
    total = None
    for part in range(2):
        high = cross_high[:, part * half : (part + 1) * half]
        low = cross_low[:, part * half : (part + 1) * half]
        wave = tables[0, :, part * lags : (part + 1) * lags]
        rest = tables[1, :, part * lags : (part + 1) * lags]
        term = mm(high, wave) + mm(low, wave) + mm(high, rest)
        total = term if part == 0 else total + term
    return total


def front_kernel(
    blocks, tables, white_re, white_im, turned
):
    devices, double, lanes = blocks.shape
    times = double // 2
    length = devices * times
    half = length // 2
    quarter = half // 2
    for part in range(2):
        data = blocks[:, part * times : (part + 1) * times, :].reshape(length, lanes)
        level = jnp.abs(data)
        edge = jnp.zeros((HALF, lanes), F32)
        tail = jnp.concatenate([level, edge], axis=0)
        total = jnp.concatenate([edge, level, edge], axis=0)
        size = length + 2 * HALF
        for step in (1, 2, 4, 8, 16):
            total = total + pltpu.roll(total, size - step, 0)
        amplitude = (total[:length] + tail[HALF:]) / (2 * HALF + 1)
        normal = data / jnp.maximum(amplitude, AMPLITUDE_FLOOR)
        turned[part * lanes : (part + 1) * lanes, :] = normal.T
    waves = [tables[n * half : (n + 1) * half, :] for n in range(4)]
    band = [tables[4 * half :, :quarter], tables[4 * half :, quarter:]]
    first = turned[:, :half]
    second = turned[:, half:]
    for parity in range(2):
        folded = first + second if parity == 0 else first - second
        high, low = split(folded)
        spectrum = (
            mm(high, waves[2 * parity])
            + mm(low, waves[2 * parity])
            + mm(high, waves[2 * parity + 1])
        )
        white_re[:, parity * quarter : (parity + 1) * quarter] = spectrum[:, :quarter]
        white_im[:, parity * quarter : (parity + 1) * quarter] = spectrum[:, quarter:]
    re = white_re[...]
    im = white_im[...]
    high, low = split(jnp.sqrt(re * re + im * im))
    for parity in range(2):
        near = slice(parity * quarter, (parity + 1) * quarter)
        other = slice((1 - parity) * quarter, (2 - parity) * quarter)
        cross_mm = mm_turned if parity else mm
        smooth = (
            mm(high[:, near], band[0])
            + mm(low[:, near], band[0])
            + cross_mm(high[:, other], band[1])
            + cross_mm(low[:, other], band[1])
        )
        gain = 1.0 / (smooth / (2 * (length // 32) + 1) + WHITE_EPSILON)
        white_re[:, near] = re[:, near] * gain
        white_im[:, near] = im[:, near] * gain


def stack_kernel(kind, white_re, white_im, tables, *refs):
    cross_high, cross_low, both = refs[-3:]
    win = lax.axis_index("win")
    z_hi, core = lax.div(win, 2), lax.rem(win, 2)
    step = {"far": 2, "ahead": 1 + 2 * core, "behind": 3 - 2 * core, "here": 0}[kind]
    correlate(white_re, white_im, cross_high, cross_low, lax.rem(z_hi + step, 4), 32)
    both[...] = invert(cross_high, cross_low, tables).reshape(both.shape)
    if kind == "behind":
        refs[-4][0] = both[1 - core]
        refs[-4][1] = both[core]
    else:
        refs[-5][...] = both[core]
        refs[-4][...] = both[1 - core]


def add_kernel(*refs):
    half = len(refs) // 3
    for left, right, out in zip(refs[:half], refs[half : 2 * half], refs[2 * half :]):
        out[...] = left[...] + right[...]


def join_kernel(own, other, received, own_sum, other_sum):
    own_sum[...] = own[...] + received[0]
    other_sum[...] = other[...] + received[1]


def local(records, sources):
    chan_count = lax.axis_size("chan")
    windows, times, channels = records.shape
    length = times * chan_count
    lag_count = length // 4
    half = length // 2
    total_windows = windows * lax.axis_size("win")
    factor = 1.0 / math.sqrt(total_windows * half)
    vmem = pl.BlockSpec(memory_space=pltpu.VMEM)
    smem = pl.BlockSpec(memory_space=pltpu.SMEM)
    hbm = pl.BlockSpec(memory_space=pltpu.HBM)
    tiles = channels // LANES

    packed = pl.pallas_call(
        pack_kernel,
        out_shape=jax.ShapeDtypeStruct((chan_count, 2 * times, LANES), F32),
        in_specs=[smem, vmem],
        out_specs=vmem,
        compiler_params=pltpu.CompilerParams(vmem_limit_bytes=4 << 20),
        name="pack",
    )(sources, records)
    blocks = lax.all_to_all(packed, "chan", 0, 0, tiled=True)

    forward = jnp.asarray(front_tables(length, length // 32))
    inverse = jnp.asarray(inverse_tables(length, lag_count, factor))
    rows = 2 * LANES
    shape = jax.ShapeDtypeStruct
    white_re, white_im = pl.pallas_call(
        front_kernel,
        out_shape=(shape((rows, half), F32), shape((rows, half), F32)),
        in_specs=[vmem] * 2,
        out_specs=(vmem, vmem),
        scratch_shapes=[pltpu.VMEM((rows, length), F32)],
        compiler_params=pltpu.CompilerParams(vmem_limit_bytes=24 << 20),
        name="front",
    )(blocks, forward)

    piece = shape((LANES, lag_count), F32)

    def stack(kind, after=None, handed=None):
        extra = [] if after is None else [after]
        outs = [shape((2, LANES, lag_count), F32)] if kind == "behind" else [piece, piece]
        aliases = {}
        if handed is not None:
            aliases = {3 + len(extra): 0}
            extra.append(handed)
            outs.insert(0, shape(handed.shape, F32))
        return pl.pallas_call(
            functools.partial(stack_kernel, kind),
            out_shape=outs,
            in_specs=[vmem] * (3 + len(extra)),
            out_specs=[vmem] * len(outs),
            scratch_shapes=[
                pltpu.VMEM((2 * LANES, length), BF16),
                pltpu.VMEM((2 * LANES, length), BF16),
                pltpu.VMEM((2, LANES, lag_count), F32),
            ],
            input_output_aliases=aliases,
            compiler_params=pltpu.CompilerParams(vmem_limit_bytes=16 << 20),
            cost_estimate=pl.CostEstimate(flops=1 << 32, bytes_accessed=1 << 24, transcendentals=0),
            name="stack_" + kind,
        )(white_re, white_im, inverse, *extra)

    def small(kernel, outs, name, *operands):
        return pl.pallas_call(
            kernel,
            out_shape=[piece] * outs,
            in_specs=[vmem] * len(operands),
            out_specs=[vmem] * outs,
            compiler_params=pltpu.CompilerParams(vmem_limit_bytes=4 << 20),
            name=name,
        )(*operands)

    def onward(value):
        pairs = [(i, (i + (2 if i % 2 == 0 else -2)) % 8) for i in range(8)]
        return lax.ppermute(value, "win", pairs)

    def across(value):
        return lax.ppermute(value, "win", [(i, i ^ 1) for i in range(8)])

    keep_far, send_far = stack("far")
    keep_far, behind = stack("behind", handed=keep_far)
    (far,) = small(add_kernel, 1, "add_far", keep_far, across(send_far))
    passing = onward(far)
    own, other = stack("ahead", after=far)
    own, other = small(join_kernel, 2, "join", own, other, across(behind))
    early = onward(other)
    own, here_own, here_other = stack("here", after=other, handed=own)
    (own,) = small(add_kernel, 1, "add_passing", own, passing)
    late = onward(own)
    turned = across(here_other + early)
    result = (here_own + late) + turned
    return jnp.transpose(result.reshape(4, 32, lag_count), (0, 2, 1))


def solution(mesh):
    placed = (P("win", "chan", None), P())
    return jax.shard_map(
        local, mesh=mesh, in_specs=placed, out_specs=P("win", None, "chan"), check_vma=False
    )
```

```python
import functools
import math

import jax
import jax.numpy as jnp
import ml_dtypes
import numpy as np
from jax import lax
from jax.experimental import pallas as pl
from jax.experimental.pallas import tpu as pltpu
from jax.sharding import PartitionSpec as P

AMPLITUDE_FLOOR = 0.25
WHITE_EPSILON = 1e-06
HALF = 16
LANES = 128
F32 = jnp.float32
BF16 = jnp.bfloat16


def split_table(table):
    high = table.astype(np.float32).astype(ml_dtypes.bfloat16)
    low = (table - high.astype(np.float64)).astype(np.float32).astype(ml_dtypes.bfloat16)
    return high, low


def bin_order(half):
    return np.concatenate([np.arange(0, half, 4), np.arange(2, half, 4), np.arange(1, half, 2)])


def wave_table(length, bins, samples):
    angles = (np.arange(samples)[:, None] * bins[None, :] % length) * (2.0 * math.pi / length)
    return np.concatenate([np.cos(angles), -np.sin(angles)], axis=1)


def front_tables(length, reach):
    half = length // 2
    odd = wave_table(length, np.arange(1, half, 2), half)
    even = [wave_table(length, np.arange(start, half, 4), half // 2) for start in (0, 2)]
    bins = bin_order(half)
    band = (np.abs(bins[:, None] - bins[None, :]) <= reach).astype(ml_dtypes.bfloat16)
    waves = [*split_table(odd), *split_table(np.concatenate(even, axis=1))]
    return np.concatenate([*waves, band], axis=0)


def inverse_tables(length, lag_count, factor):
    half = length // 2
    bins = bin_order(half)
    lags = np.arange(lag_count) - lag_count // 2
    angles = (bins[:, None] * lags[None, :] % length) * (2.0 * math.pi / length)
    weights = np.where(bins == 0, 1.0, 2.0)[:, None] * factor
    return np.stack(
        split_table(np.concatenate([weights * np.cos(angles), -weights * np.sin(angles)], axis=1))
    )


def split(value):
    high = value.astype(BF16)
    return high, (value - high.astype(F32)).astype(BF16)


def mm(left, right):
    return jnp.dot(left, right, preferred_element_type=F32)


def pack_kernel(records, packed):
    windows, times, channels = records.shape
    dests = packed.shape[0]
    width = channels // dests
    per_tile = LANES // width
    lane = lax.broadcasted_iota(jnp.int32, (times, LANES), 1)
    for tile in range(channels // LANES):
        loaded = [records[w, :, tile * LANES : (tile + 1) * LANES] for w in range(windows)]
        for e in range(per_tile):
            block = None
            for w in range(windows):
                shift = (w - e) * width % LANES
                moved = pltpu.roll(loaded[w], shift, 1) if shift else loaded[w]
                block = moved if block is None else jnp.where(lane >= w * width, moved, block)
            packed[tile * per_tile + e, 0:times, :] = block


def pick_kernel(sources, records, packed_in, packed):
    windows, times, channels = records.shape
    dests = packed.shape[0]
    width = channels // dests
    per_tile = LANES // width
    lane = lax.broadcasted_iota(jnp.int32, (times, LANES), 1)
    column = lax.rem(lane, dests)
    place = jnp.zeros((times, LANES), jnp.int32)
    for s in range(dests):
        place = jnp.where(column == s, sources[s] - s * width // LANES * LANES, place)
    pick = jnp.zeros((times, LANES), F32)
    for tile in range(channels // LANES):
        for w in range(windows):
            loaded = records[w, :, tile * LANES : (tile + 1) * LANES]
            moved = jnp.take_along_axis(loaded, place, axis=1)
            low = w * dests + tile * per_tile
            pick = jnp.where((lane >= low) & (lane < low + per_tile), moved, pick)
    for d in range(dests):
        packed[d, times : 2 * times, :] = pick


def correlate(white_re, white_im, cross_high, cross_low, target, width, core=None):
    rows, half = white_re.shape
    lanes = rows // 2
    windows = lanes // width
    rows8 = [
        pl.ds(pl.multiple_of(lanes + w * width + target * 8, 8), 8) for w in range(windows)
    ]
    for tile in range(half // LANES):
        span = slice(tile * LANES, (tile + 1) * LANES)
        span2 = slice(half + tile * LANES, half + (tile + 1) * LANES)
        chan_re = [white_re[w * width : (w + 1) * width, span] for w in range(windows)]
        chan_im = [white_im[w * width : (w + 1) * width, span] for w in range(windows)]
        from_re = [white_re[at, span] for at in rows8]
        from_im = [white_im[at, span] for at in rows8]
        if core is not None:
            turn = lax.rem(8 - 4 * core, 8)
            from_re = [pltpu.roll(rows, turn, 0) for rows in from_re]
            from_im = [pltpu.roll(rows, turn, 0) for rows in from_im]
        chan_sum = [a + b for a, b in zip(chan_re, chan_im)]
        from_sum = [a + b for a, b in zip(from_re, from_im)]
        from_less = [a - b for a, b in zip(from_re, from_im)]
        for i in range(cross_high.shape[0] // width):
            for w in range(windows):
                one = jnp.broadcast_to(from_re[w][i : i + 1], (width, LANES)) * chan_sum[w]
                two = jnp.broadcast_to(from_less[w][i : i + 1], (width, LANES)) * chan_im[w]
                three = jnp.broadcast_to(from_sum[w][i : i + 1], (width, LANES)) * chan_re[w]
                ones = one if w == 0 else ones + one
                twos = two if w == 0 else twos + two
                threes = three if w == 0 else threes + three
            at = slice(i * width, (i + 1) * width)
            cross_high[at, span], cross_low[at, span] = split(ones - twos)
            cross_high[at, span2], cross_low[at, span2] = split(ones - threes)


def invert(cross_high, cross_low, tables):
    half = cross_high.shape[1] // 2
    lags = half // 2
    total = None
    for part in range(2):
        high = cross_high[:, part * half : (part + 1) * half]
        low = cross_low[:, part * half : (part + 1) * half]
        wave = tables[0, :, part * lags : (part + 1) * lags]
        rest = tables[1, :, part * lags : (part + 1) * lags]
        term = mm(high, wave) + mm(low, wave) + mm(high, rest)
        total = term if part == 0 else total + term
    return total


def level_kernel(blocks, turned):
    devices, double, lanes = blocks.shape
    times = double // 2
    length = devices * times
    for part in range(2):
        data = blocks[:, part * times : (part + 1) * times, :].reshape(length, lanes)
        level = jnp.abs(data)
        edge = jnp.zeros((HALF, lanes), F32)
        tail = jnp.concatenate([level, edge], axis=0)
        total = jnp.concatenate([edge, level, edge], axis=0)
        size = length + 2 * HALF
        for step in (1, 2, 4, 8, 16):
            total = total + pltpu.roll(total, size - step, 0)
        amplitude = (total[:length] + tail[HALF:]) * (1.0 / (2 * HALF + 1))
        normal = data / jnp.maximum(amplitude, AMPLITUDE_FLOOR)
        turned[part * lanes : (part + 1) * lanes, :] = normal.T


def spectra_kernel(turned, tables, white_re, white_im):
    length = turned.shape[1]
    half = length // 2
    quarter = half // 2
    eighth = quarter // 2

    def waves(row, rows, columns):
        return tables[row : row + rows, columns], tables[row + rows : row + 2 * rows, columns]

    def transform(data, table):
        high, low = split(data)
        return mm(high, table[0]) + mm(low, table[0]) + mm(high, table[1])

    first, second = turned[:, :half], turned[:, half:]
    odd = transform(first - second, waves(0, half, slice(0, half)))
    folded = first + second
    first, second = folded[:, :quarter], folded[:, quarter:]
    zero = transform(first + second, waves(length, quarter, slice(0, quarter)))
    two = transform(first - second, waves(length, quarter, slice(quarter, half)))
    re = jnp.concatenate([zero[:, :eighth], two[:, :eighth], odd[:, :quarter]], axis=1)
    im = jnp.concatenate([zero[:, eighth:], two[:, eighth:], odd[:, quarter:]], axis=1)
    high, low = split(jnp.sqrt(re * re + im * im))
    band = tables[length + half :, :]
    smooth = (mm(high, band) + mm(low, band)) * (1.0 / (2 * (length // 32) + 1))
    gain = 1.0 / (smooth + WHITE_EPSILON)
    white_re[...] = re * gain
    white_im[...] = im * gain


def stack_kernel(kind, white_re, white_im, tables, *refs):
    win = lax.axis_index("win")
    z_hi, core = lax.div(win, 2), lax.rem(win, 2)
    if kind.startswith("far"):
        result, cross_high, cross_low = refs[-3:]
        which = core if kind == "far_keep" else 1 - core
        target = lax.rem(z_hi + 2, 4)
        correlate(white_re, white_im, cross_high, cross_low, target, 32, which)
        result[...] = invert(cross_high, cross_low, tables)
        return
    cross_high, cross_low, both = refs[-3:]
    step = {"ahead": 1 + 2 * core, "behind": 3 - 2 * core, "here": 0}[kind]
    correlate(white_re, white_im, cross_high, cross_low, lax.rem(z_hi + step, 4), 32)
    both[...] = invert(cross_high, cross_low, tables).reshape(both.shape)
    if kind == "behind":
        refs[-4][0] = both[1 - core]
        refs[-4][1] = both[core]
    else:
        refs[-5][...] = both[core]
        refs[-4][...] = both[1 - core]


def add_kernel(*refs):
    half = len(refs) // 3
    for left, right, out in zip(refs[:half], refs[half : 2 * half], refs[2 * half :]):
        out[...] = left[...] + right[...]


def join_kernel(own, other, received, own_sum, other_sum):
    own_sum[...] = own[...] + received[0]
    other_sum[...] = other[...] + received[1]


def local(records, sources):
    chan_count = lax.axis_size("chan")
    windows, times, channels = records.shape
    length = times * chan_count
    lag_count = length // 4
    half = length // 2
    total_windows = windows * lax.axis_size("win")
    factor = 1.0 / math.sqrt(total_windows * half)
    vmem = pl.BlockSpec(memory_space=pltpu.VMEM)
    smem = pl.BlockSpec(memory_space=pltpu.SMEM)

    block_shape = jax.ShapeDtypeStruct((chan_count, 2 * times, LANES), F32)
    packed = pl.pallas_call(
        pack_kernel,
        out_shape=block_shape,
        in_specs=[vmem],
        out_specs=vmem,
        compiler_params=pltpu.CompilerParams(vmem_limit_bytes=4 << 20),
        cost_estimate=pl.CostEstimate(flops=1 << 31, bytes_accessed=1 << 20, transcendentals=0),
        name="pack",
    )(records)
    packed = pl.pallas_call(
        pick_kernel,
        out_shape=block_shape,
        in_specs=[smem, vmem, vmem],
        out_specs=vmem,
        input_output_aliases={2: 0},
        compiler_params=pltpu.CompilerParams(vmem_limit_bytes=4 << 20),
        name="pick",
    )(sources, records, packed)
    blocks = lax.all_to_all(packed, "chan", 0, 0, tiled=True)

    forward = jnp.asarray(front_tables(length, length // 32))
    inverse = jnp.asarray(inverse_tables(length, lag_count, factor))
    rows = 2 * LANES
    shape = jax.ShapeDtypeStruct
    turned = pl.pallas_call(
        level_kernel,
        out_shape=shape((rows, length), F32),
        in_specs=[vmem],
        out_specs=vmem,
        compiler_params=pltpu.CompilerParams(vmem_limit_bytes=16 << 20),
        cost_estimate=pl.CostEstimate(flops=1 << 28, bytes_accessed=1 << 20, transcendentals=0),
        name="level",
    )(blocks)
    white_re, white_im = pl.pallas_call(
        spectra_kernel,
        out_shape=(shape((rows, half), F32), shape((rows, half), F32)),
        in_specs=[vmem] * 2,
        out_specs=(vmem, vmem),
        compiler_params=pltpu.CompilerParams(vmem_limit_bytes=24 << 20),
        cost_estimate=pl.CostEstimate(flops=1 << 32, bytes_accessed=1 << 24, transcendentals=0),
        name="spectra",
    )(turned, forward)

    piece = shape((LANES, lag_count), F32)

    def stack(kind, after=None, handed=None):
        extra = [] if after is None else [after]
        outs = {
            "behind": [shape((2, LANES, lag_count), F32)],
            "far_send": [piece],
            "far_keep": [piece],
        }.get(kind, [piece, piece])
        rows = LANES if kind.startswith("far") else 2 * LANES
        scratch = [pltpu.VMEM((rows, length), BF16), pltpu.VMEM((rows, length), BF16)]
        if rows > LANES:
            scratch.append(pltpu.VMEM((2, LANES, lag_count), F32))
        aliases = {}
        if handed is not None:
            aliases = {3 + len(extra): 0}
            extra.append(handed)
            outs.insert(0, shape(handed.shape, F32))
        return pl.pallas_call(
            functools.partial(stack_kernel, kind),
            out_shape=outs,
            in_specs=[vmem] * (3 + len(extra)),
            out_specs=[vmem] * len(outs),
            scratch_shapes=scratch,
            input_output_aliases=aliases,
            compiler_params=pltpu.CompilerParams(vmem_limit_bytes=16 << 20),
            cost_estimate=pl.CostEstimate(flops=1 << 32, bytes_accessed=1 << 24, transcendentals=0),
            name="stack_" + kind,
        )(white_re, white_im, inverse, *extra)

    def small(kernel, outs, name, *operands):
        return pl.pallas_call(
            kernel,
            out_shape=[piece] * outs,
            in_specs=[vmem] * len(operands),
            out_specs=[vmem] * outs,
            compiler_params=pltpu.CompilerParams(vmem_limit_bytes=4 << 20),
            name=name,
        )(*operands)

    def onward(value):
        pairs = [(i, (i + (2 if i % 2 == 0 else -2)) % 8) for i in range(8)]
        return lax.ppermute(value, "win", pairs)

    def across(value):
        return lax.ppermute(value, "win", [(i, i ^ 1) for i in range(8)])

    (send_far,) = stack("far_send")
    (keep_far,) = stack("far_keep", after=send_far)
    (far,) = small(add_kernel, 1, "add_far", keep_far, across(send_far))
    passing = onward(far)
    (behind,) = stack("behind", after=far)
    own, other = stack("ahead", after=behind)
    own, other = small(join_kernel, 2, "join", own, other, across(behind))
    early = onward(other)
    own, here_own, here_other = stack("here", after=other, handed=own)
    (own,) = small(add_kernel, 1, "add_passing", own, passing)
    late = onward(own)
    turned = across(here_other + early)
    result = (here_own + late) + turned
    return jnp.transpose(result.reshape(4, 32, lag_count), (0, 2, 1))


def solution(mesh):
    placed = (P("win", "chan", None), P())
    return jax.shard_map(
        local, mesh=mesh, in_specs=placed, out_specs=P("win", None, "chan"), check_vma=False
    )
```

```python
import functools
import math

import jax
import jax.numpy as jnp
import ml_dtypes
import numpy as np
from jax import lax
from jax.experimental import pallas as pl
from jax.experimental.pallas import tpu as pltpu
from jax.sharding import PartitionSpec as P

AMPLITUDE_FLOOR = 0.25
WHITE_EPSILON = 1e-06
HALF = 16
LANES = 128
F32 = jnp.float32
BF16 = jnp.bfloat16


def split_table(table):
    high = table.astype(np.float32).astype(ml_dtypes.bfloat16)
    low = (table - high.astype(np.float64)).astype(np.float32).astype(ml_dtypes.bfloat16)
    return high, low


def bin_order(half):
    return np.concatenate([np.arange(0, half, 4), np.arange(2, half, 4), np.arange(1, half, 2)])


def wave_table(length, bins, samples):
    angles = (np.arange(samples)[:, None] * bins[None, :] % length) * (2.0 * math.pi / length)
    return np.concatenate([np.cos(angles), -np.sin(angles)], axis=1)


def front_tables(length, reach):
    half = length // 2
    odd = wave_table(length, np.arange(1, half, 2), half)
    even = [wave_table(length, np.arange(start, half, 4), half // 2) for start in (0, 2)]
    bins = bin_order(half)
    band = (np.abs(bins[:, None] - bins[None, :]) <= reach).astype(ml_dtypes.bfloat16)
    waves = [*split_table(odd), *split_table(np.concatenate(even, axis=1))]
    return np.concatenate([*waves, band], axis=0)


def inverse_tables(length, lag_count, factor):
    half = length // 2
    bins = bin_order(half)
    lags = np.arange(lag_count) - lag_count // 2
    angles = (bins[:, None] * lags[None, :] % length) * (2.0 * math.pi / length)
    weights = np.where(bins == 0, 1.0, 2.0)[:, None] * factor
    return np.stack(
        split_table(np.concatenate([weights * np.cos(angles), -weights * np.sin(angles)], axis=1))
    )


def split(value):
    high = value.astype(BF16)
    return high, (value - high.astype(F32)).astype(BF16)


def mm(left, right):
    return jnp.dot(left, right, preferred_element_type=F32)


def pack_kernel(records, packed):
    windows, times, channels = records.shape
    dests = packed.shape[0]
    width = channels // dests
    per_tile = LANES // width
    lane = lax.broadcasted_iota(jnp.int32, (times, LANES), 1)
    for tile in range(channels // LANES):
        loaded = [records[w, :, tile * LANES : (tile + 1) * LANES] for w in range(windows)]
        for e in range(per_tile):
            block = None
            for w in range(windows):
                shift = (w - e) * width % LANES
                moved = pltpu.roll(loaded[w], shift, 1) if shift else loaded[w]
                block = moved if block is None else jnp.where(lane >= w * width, moved, block)
            packed[tile * per_tile + e, 0:times, :] = block


def pick_kernel(sources, records, packed_in, packed):
    windows, times, channels = records.shape
    dests = packed.shape[0]
    width = channels // dests
    per_tile = LANES // width
    lane = lax.broadcasted_iota(jnp.int32, (times, LANES), 1)
    place = jnp.concatenate([sources[...]] * windows, axis=1) & (LANES - 1)
    place = jnp.broadcast_to(place, (times, LANES))
    pick = jnp.zeros((times, LANES), F32)
    for tile in range(channels // LANES):
        for w in range(windows):
            loaded = records[w, :, tile * LANES : (tile + 1) * LANES]
            moved = jnp.take_along_axis(loaded, place, axis=1)
            low = w * dests + tile * per_tile
            pick = jnp.where((lane >= low) & (lane < low + per_tile), moved, pick)
    for d in range(dests):
        packed[d, times : 2 * times, :] = pick


def correlate(white_re, white_im, cross_high, cross_low, target, width, core=None):
    rows, half = white_re.shape
    lanes = rows // 2
    windows = lanes // width
    rows8 = [
        pl.ds(pl.multiple_of(lanes + w * width + target * 8, 8), 8) for w in range(windows)
    ]
    for tile in range(half // LANES):
        span = slice(tile * LANES, (tile + 1) * LANES)
        span2 = slice(half + tile * LANES, half + (tile + 1) * LANES)
        chan_re = [white_re[w * width : (w + 1) * width, span] for w in range(windows)]
        chan_im = [white_im[w * width : (w + 1) * width, span] for w in range(windows)]
        from_re = [white_re[at, span] for at in rows8]
        from_im = [white_im[at, span] for at in rows8]
        if core is not None:
            turn = lax.rem(8 - 4 * core, 8)
            from_re = [pltpu.roll(rows, turn, 0) for rows in from_re]
            from_im = [pltpu.roll(rows, turn, 0) for rows in from_im]
        chan_sum = [a + b for a, b in zip(chan_re, chan_im)]
        from_sum = [a + b for a, b in zip(from_re, from_im)]
        from_less = [a - b for a, b in zip(from_re, from_im)]
        for i in range(cross_high.shape[0] // width):
            for w in range(windows):
                one = jnp.broadcast_to(from_re[w][i : i + 1], (width, LANES)) * chan_sum[w]
                two = jnp.broadcast_to(from_less[w][i : i + 1], (width, LANES)) * chan_im[w]
                three = jnp.broadcast_to(from_sum[w][i : i + 1], (width, LANES)) * chan_re[w]
                ones = one if w == 0 else ones + one
                twos = two if w == 0 else twos + two
                threes = three if w == 0 else threes + three
            at = slice(i * width, (i + 1) * width)
            cross_high[at, span], cross_low[at, span] = split(ones - twos)
            cross_high[at, span2], cross_low[at, span2] = split(ones - threes)


def invert(cross_high, cross_low, tables):
    half = cross_high.shape[1] // 2
    lags = half // 2
    total = None
    for part in range(2):
        high = cross_high[:, part * half : (part + 1) * half]
        low = cross_low[:, part * half : (part + 1) * half]
        wave = tables[0, :, part * lags : (part + 1) * lags]
        rest = tables[1, :, part * lags : (part + 1) * lags]
        term = mm(high, wave) + mm(low, wave) + mm(high, rest)
        total = term if part == 0 else total + term
    return total


def level_kernel(blocks, turned):
    devices, double, lanes = blocks.shape
    times = double // 2
    length = devices * times
    for part in range(2):
        data = blocks[:, part * times : (part + 1) * times, :].reshape(length, lanes)
        level = jnp.abs(data)
        edge = jnp.zeros((HALF, lanes), F32)
        tail = jnp.concatenate([level, edge], axis=0)
        total = jnp.concatenate([edge, level, edge], axis=0)
        size = length + 2 * HALF
        for step in (1, 2, 4, 8, 16):
            total = total + pltpu.roll(total, size - step, 0)
        amplitude = (total[:length] + tail[HALF:]) * (1.0 / (2 * HALF + 1))
        normal = data / jnp.maximum(amplitude, AMPLITUDE_FLOOR)
        turned[part * lanes : (part + 1) * lanes, :] = normal.T


def spectra_kernel(turned, tables, white_re, white_im):
    length = turned.shape[1]
    half = length // 2
    quarter = half // 2
    eighth = quarter // 2

    def waves(row, rows, columns):
        return tables[row : row + rows, columns], tables[row + rows : row + 2 * rows, columns]

    def transform(data, table):
        high, low = split(data)
        return mm(high, table[0]) + mm(low, table[0]) + mm(high, table[1])

    first, second = turned[:, :half], turned[:, half:]
    odd = transform(first - second, waves(0, half, slice(0, half)))
    folded = first + second
    first, second = folded[:, :quarter], folded[:, quarter:]
    zero = transform(first + second, waves(length, quarter, slice(0, quarter)))
    two = transform(first - second, waves(length, quarter, slice(quarter, half)))
    re = jnp.concatenate([zero[:, :eighth], two[:, :eighth], odd[:, :quarter]], axis=1)
    im = jnp.concatenate([zero[:, eighth:], two[:, eighth:], odd[:, quarter:]], axis=1)
    high, low = split(jnp.sqrt(re * re + im * im))
    band = tables[length + half :, :]
    smooth = (mm(high, band) + mm(low, band)) * (1.0 / (2 * (length // 32) + 1))
    gain = 1.0 / (smooth + WHITE_EPSILON)
    white_re[...] = re * gain
    white_im[...] = im * gain


def stack_kernel(kind, white_re, white_im, tables, *refs):
    win = lax.axis_index("win")
    z_hi, core = lax.div(win, 2), lax.rem(win, 2)
    if kind.startswith(("far", "here")):
        result, cross_high, cross_low = refs[-3:]
        which = core if kind.endswith("own") else 1 - core
        target = lax.rem(z_hi + (2 if kind.startswith("far") else 0), 4)
        correlate(white_re, white_im, cross_high, cross_low, target, 32, which)
        result[...] = invert(cross_high, cross_low, tables)
        return
    cross_high, cross_low, both = refs[-3:]
    step = {"ahead": 1 + 2 * core, "behind": 3 - 2 * core}[kind]
    correlate(white_re, white_im, cross_high, cross_low, lax.rem(z_hi + step, 4), 32)
    both[...] = invert(cross_high, cross_low, tables).reshape(both.shape)
    if kind == "behind":
        refs[-4][0] = both[1 - core]
        refs[-4][1] = both[core]
    else:
        refs[-5][...] = both[core]
        refs[-4][...] = both[1 - core]


def add_kernel(*refs):
    half = len(refs) // 3
    for left, right, out in zip(refs[:half], refs[half : 2 * half], refs[2 * half :]):
        out[...] = left[...] + right[...]


def join_kernel(own, other, received, own_sum, other_sum):
    own_sum[...] = own[...] + received[0]
    other_sum[...] = other[...] + received[1]


def local(records, sources):
    chan_count = lax.axis_size("chan")
    windows, times, channels = records.shape
    length = times * chan_count
    lag_count = length // 4
    half = length // 2
    total_windows = windows * lax.axis_size("win")
    factor = 1.0 / math.sqrt(total_windows * half)
    vmem = pl.BlockSpec(memory_space=pltpu.VMEM)

    block_shape = jax.ShapeDtypeStruct((chan_count, 2 * times, LANES), F32)
    packed = pl.pallas_call(
        pack_kernel,
        out_shape=block_shape,
        in_specs=[vmem],
        out_specs=vmem,
        compiler_params=pltpu.CompilerParams(vmem_limit_bytes=4 << 20),
        cost_estimate=pl.CostEstimate(flops=1 << 31, bytes_accessed=1 << 20, transcendentals=0),
        name="pack",
    )(records)
    packed = pl.pallas_call(
        pick_kernel,
        out_shape=block_shape,
        in_specs=[vmem, vmem, vmem],
        out_specs=vmem,
        input_output_aliases={2: 0},
        compiler_params=pltpu.CompilerParams(vmem_limit_bytes=4 << 20),
        name="pick",
    )(sources.reshape(1, -1), records, packed)
    blocks = lax.all_to_all(packed, "chan", 0, 0, tiled=True)

    forward = jnp.asarray(front_tables(length, length // 32))
    inverse = jnp.asarray(inverse_tables(length, lag_count, factor))
    rows = 2 * LANES
    shape = jax.ShapeDtypeStruct
    turned = pl.pallas_call(
        level_kernel,
        out_shape=shape((rows, length), F32),
        in_specs=[vmem],
        out_specs=vmem,
        compiler_params=pltpu.CompilerParams(vmem_limit_bytes=16 << 20),
        cost_estimate=pl.CostEstimate(flops=1 << 28, bytes_accessed=1 << 20, transcendentals=0),
        name="level",
    )(blocks)
    white_re, white_im = pl.pallas_call(
        spectra_kernel,
        out_shape=(shape((rows, half), F32), shape((rows, half), F32)),
        in_specs=[vmem] * 2,
        out_specs=(vmem, vmem),
        compiler_params=pltpu.CompilerParams(vmem_limit_bytes=24 << 20),
        cost_estimate=pl.CostEstimate(flops=1 << 32, bytes_accessed=1 << 24, transcendentals=0),
        name="spectra",
    )(turned, forward)

    piece = shape((LANES, lag_count), F32)

    def stack(kind, after=None, handed=None):
        extra = [] if after is None else [after]
        outs = {
            "behind": [shape((2, LANES, lag_count), F32)],
            "ahead": [piece, piece],
        }.get(kind, [piece])
        rows = 2 * LANES if kind in ("behind", "ahead") else LANES
        scratch = [pltpu.VMEM((rows, length), BF16), pltpu.VMEM((rows, length), BF16)]
        if rows > LANES:
            scratch.append(pltpu.VMEM((2, LANES, lag_count), F32))
        aliases = {}
        if handed is not None:
            aliases = {3 + len(extra): 0}
            extra.append(handed)
            outs.insert(0, shape(handed.shape, F32))
        return pl.pallas_call(
            functools.partial(stack_kernel, kind),
            out_shape=outs,
            in_specs=[vmem] * (3 + len(extra)),
            out_specs=[vmem] * len(outs),
            scratch_shapes=scratch,
            input_output_aliases=aliases,
            compiler_params=pltpu.CompilerParams(vmem_limit_bytes=16 << 20),
            cost_estimate=pl.CostEstimate(flops=1 << 32, bytes_accessed=1 << 24, transcendentals=0),
            name="stack_" + kind,
        )(white_re, white_im, inverse, *extra)

    def small(kernel, outs, name, *operands):
        return pl.pallas_call(
            kernel,
            out_shape=[piece] * outs,
            in_specs=[vmem] * len(operands),
            out_specs=[vmem] * outs,
            compiler_params=pltpu.CompilerParams(vmem_limit_bytes=4 << 20),
            name=name,
        )(*operands)

    def onward(value):
        pairs = [(i, (i + (2 if i % 2 == 0 else -2)) % 8) for i in range(8)]
        return lax.ppermute(value, "win", pairs)

    def across(value):
        return lax.ppermute(value, "win", [(i, i ^ 1) for i in range(8)])

    (send_far,) = stack("far_other")
    (keep_far,) = stack("far_own", after=send_far)
    (far,) = small(add_kernel, 1, "add_far", keep_far, across(send_far))
    passing = onward(far)
    (behind,) = stack("behind", after=far)
    own, other = stack("ahead", after=behind)
    own, other = small(join_kernel, 2, "join", own, other, across(behind))
    early = onward(other)
    (own,) = small(add_kernel, 1, "add_passing", own, passing)
    late = onward(own)
    (here_own,) = stack("here_own", after=own)
    (here_other,) = stack("here_other", after=early)
    turned = across(here_other + early)
    result = (here_own + late) + turned
    return jnp.transpose(result.reshape(4, 32, lag_count), (0, 2, 1))


def solution(mesh):
    placed = (P("win", "chan", None), P())
    return jax.shard_map(
        local, mesh=mesh, in_specs=placed, out_specs=P("win", None, "chan"), check_vma=False
    )
```

```python
import functools
import math

import jax
import jax.numpy as jnp
import ml_dtypes
import numpy as np
from jax import lax
from jax.experimental import pallas as pl
from jax.experimental.pallas import tpu as pltpu
from jax.sharding import PartitionSpec as P

AMPLITUDE_FLOOR = 0.25
WHITE_EPSILON = 1e-06
HALF = 16
LANES = 128
F32 = jnp.float32
BF16 = jnp.bfloat16


def split_table(table):
    high = table.astype(np.float32).astype(ml_dtypes.bfloat16)
    low = (table - high.astype(np.float64)).astype(np.float32).astype(ml_dtypes.bfloat16)
    return high, low


def bin_order(half):
    return np.concatenate([np.arange(0, half, 4), np.arange(2, half, 4), np.arange(1, half, 2)])


def wave_table(length, bins, samples):
    angles = (np.arange(samples)[:, None] * bins[None, :] % length) * (2.0 * math.pi / length)
    return np.concatenate([np.cos(angles), -np.sin(angles)], axis=1)


def front_tables(length, reach):
    half = length // 2
    odd = wave_table(length, np.arange(1, half, 2), half)
    even = [wave_table(length, np.arange(start, half, 4), half // 2) for start in (0, 2)]
    bins = bin_order(half)
    band = (np.abs(bins[:, None] - bins[None, :]) <= reach).astype(ml_dtypes.bfloat16)
    waves = [*split_table(odd), *split_table(np.concatenate(even, axis=1))]
    return np.concatenate([*waves, band], axis=0)


def inverse_tables(length, lag_count, factor):
    half = length // 2
    bins = bin_order(half)
    lags = np.arange(lag_count) - lag_count // 2
    angles = (bins[:, None] * lags[None, :] % length) * (2.0 * math.pi / length)
    weights = np.where(bins == 0, 1.0, 2.0)[:, None] * factor
    return np.stack(
        split_table(np.concatenate([weights * np.cos(angles), -weights * np.sin(angles)], axis=1))
    )


def split(value):
    high = value.astype(BF16)
    return high, (value - high.astype(F32)).astype(BF16)


def mm(left, right):
    return jnp.dot(left, right, preferred_element_type=F32)


def pack_kernel(records, packed):
    windows, times, channels = records.shape
    dests = packed.shape[0]
    width = channels // dests
    per_tile = LANES // width
    lane = lax.broadcasted_iota(jnp.int32, (times, LANES), 1)
    for tile in range(channels // LANES):
        loaded = [records[w, :, tile * LANES : (tile + 1) * LANES] for w in range(windows)]
        for e in range(per_tile):
            block = None
            for w in range(windows):
                shift = (w - e) * width % LANES
                moved = pltpu.roll(loaded[w], shift, 1) if shift else loaded[w]
                block = moved if block is None else jnp.where(lane >= w * width, moved, block)
            packed[tile * per_tile + e, 0:times, :] = block


def pick_kernel(sources, records, packed_in, packed):
    windows, times, channels = records.shape
    dests = packed.shape[0]
    width = channels // dests
    per_tile = LANES // width
    lane = lax.broadcasted_iota(jnp.int32, (times, LANES), 1)
    place = jnp.concatenate([sources[...]] * windows, axis=1) & (LANES - 1)
    place = jnp.broadcast_to(place, (times, LANES))
    pick = jnp.zeros((times, LANES), F32)
    for tile in range(channels // LANES):
        for w in range(windows):
            loaded = records[w, :, tile * LANES : (tile + 1) * LANES]
            moved = jnp.take_along_axis(loaded, place, axis=1)
            low = w * dests + tile * per_tile
            pick = jnp.where((lane >= low) & (lane < low + per_tile), moved, pick)
    for d in range(dests):
        packed[d, times : 2 * times, :] = pick


def correlate(white_re, white_im, cross_high, cross_low, target, width, core=None):
    rows, half = white_re.shape
    lanes = rows // 2
    windows = lanes // width
    rows8 = [
        pl.ds(pl.multiple_of(lanes + w * width + target * 8, 8), 8) for w in range(windows)
    ]
    for tile in range(half // LANES):
        span = slice(tile * LANES, (tile + 1) * LANES)
        span2 = slice(half + tile * LANES, half + (tile + 1) * LANES)
        chan_re = [white_re[w * width : (w + 1) * width, span] for w in range(windows)]
        chan_im = [white_im[w * width : (w + 1) * width, span] for w in range(windows)]
        from_re = [white_re[at, span] for at in rows8]
        from_im = [white_im[at, span] for at in rows8]
        if core is not None:
            turn = lax.rem(8 - 4 * core, 8)
            from_re = [pltpu.roll(rows, turn, 0) for rows in from_re]
            from_im = [pltpu.roll(rows, turn, 0) for rows in from_im]
        chan_sum = [a + b for a, b in zip(chan_re, chan_im)]
        from_sum = [a + b for a, b in zip(from_re, from_im)]
        from_less = [a - b for a, b in zip(from_re, from_im)]
        for i in range(cross_high.shape[0] // width):
            for w in range(windows):
                one = jnp.broadcast_to(from_re[w][i : i + 1], (width, LANES)) * chan_sum[w]
                two = jnp.broadcast_to(from_less[w][i : i + 1], (width, LANES)) * chan_im[w]
                three = jnp.broadcast_to(from_sum[w][i : i + 1], (width, LANES)) * chan_re[w]
                ones = one if w == 0 else ones + one
                twos = two if w == 0 else twos + two
                threes = three if w == 0 else threes + three
            at = slice(i * width, (i + 1) * width)
            cross_high[at, span], cross_low[at, span] = split(ones - twos)
            cross_high[at, span2], cross_low[at, span2] = split(ones - threes)


def invert(cross_high, cross_low, tables):
    half = cross_high.shape[1] // 2
    lags = half // 2
    total = None
    for part in range(2):
        high = cross_high[:, part * half : (part + 1) * half]
        low = cross_low[:, part * half : (part + 1) * half]
        wave = tables[0, :, part * lags : (part + 1) * lags]
        rest = tables[1, :, part * lags : (part + 1) * lags]
        term = mm(high, wave) + mm(low, wave) + mm(high, rest)
        total = term if part == 0 else total + term
    return total


def level_kernel(blocks, turned):
    devices, double, lanes = blocks.shape
    times = double // 2
    length = devices * times
    for part in range(2):
        data = blocks[:, part * times : (part + 1) * times, :].reshape(length, lanes)
        level = jnp.abs(data)
        edge = jnp.zeros((HALF, lanes), F32)
        tail = jnp.concatenate([level, edge], axis=0)
        total = jnp.concatenate([edge, level, edge], axis=0)
        size = length + 2 * HALF
        for step in (1, 2, 4, 8, 16):
            total = total + pltpu.roll(total, size - step, 0)
        amplitude = (total[:length] + tail[HALF:]) * (1.0 / (2 * HALF + 1))
        normal = data / jnp.maximum(amplitude, AMPLITUDE_FLOOR)
        turned[part * lanes : (part + 1) * lanes, :] = normal.T


def spectra_kernel(turned, tables, white_re, white_im):
    length = turned.shape[1]
    half = length // 2
    quarter = half // 2
    eighth = quarter // 2

    def waves(row, rows, columns):
        return tables[row : row + rows, columns], tables[row + rows : row + 2 * rows, columns]

    def transform(data, table):
        high, low = split(data)
        return mm(high, table[0]) + mm(low, table[0]) + mm(high, table[1])

    first, second = turned[:, :half], turned[:, half:]
    odd = transform(first - second, waves(0, half, slice(0, half)))
    folded = first + second
    first, second = folded[:, :quarter], folded[:, quarter:]
    zero = transform(first + second, waves(length, quarter, slice(0, quarter)))
    two = transform(first - second, waves(length, quarter, slice(quarter, half)))
    re = jnp.concatenate([zero[:, :eighth], two[:, :eighth], odd[:, :quarter]], axis=1)
    im = jnp.concatenate([zero[:, eighth:], two[:, eighth:], odd[:, quarter:]], axis=1)
    high, low = split(jnp.sqrt(re * re + im * im))
    band = tables[length + half :, :]
    smooth = (mm(high, band) + mm(low, band)) * (1.0 / (2 * (length // 32) + 1))
    gain = 1.0 / (smooth + WHITE_EPSILON)
    white_re[...] = re * gain
    white_im[...] = im * gain


def stack_kernel(kind, white_re, white_im, tables, *refs):
    win = lax.axis_index("win")
    z_hi, core = lax.div(win, 2), lax.rem(win, 2)
    if kind.startswith(("far", "here")):
        result, cross_high, cross_low = refs[-3:]
        which = core if kind.endswith("own") else 1 - core
        target = lax.rem(z_hi + (2 if kind.startswith("far") else 0), 4)
        correlate(white_re, white_im, cross_high, cross_low, target, 32, which)
        result[...] = invert(cross_high, cross_low, tables)
        return
    cross_high, cross_low, both = refs[-3:]
    step = {"ahead": 1 + 2 * core, "behind": 3 - 2 * core}[kind]
    correlate(white_re, white_im, cross_high, cross_low, lax.rem(z_hi + step, 4), 32)
    both[...] = invert(cross_high, cross_low, tables).reshape(both.shape)
    if kind == "behind":
        refs[-4][0] = both[1 - core]
        refs[-4][1] = both[core]
    else:
        refs[-5][...] = both[core]
        refs[-4][...] = both[1 - core]


def add_kernel(*refs):
    half = len(refs) // 3
    for left, right, out in zip(refs[:half], refs[half : 2 * half], refs[2 * half :]):
        out[...] = left[...] + right[...]


def join_kernel(own, other, received, own_sum, other_sum):
    own_sum[...] = own[...] + received[0]
    other_sum[...] = other[...] + received[1]


def local(records, sources):
    chan_count = lax.axis_size("chan")
    windows, times, channels = records.shape
    length = times * chan_count
    lag_count = length // 4
    half = length // 2
    total_windows = windows * lax.axis_size("win")
    factor = 1.0 / math.sqrt(total_windows * half)
    vmem = pl.BlockSpec(memory_space=pltpu.VMEM)

    block_shape = jax.ShapeDtypeStruct((chan_count, 2 * times, LANES), F32)
    packed = pl.pallas_call(
        pack_kernel,
        out_shape=block_shape,
        in_specs=[vmem],
        out_specs=vmem,
        compiler_params=pltpu.CompilerParams(vmem_limit_bytes=4 << 20),
        cost_estimate=pl.CostEstimate(flops=1 << 31, bytes_accessed=1 << 20, transcendentals=0),
        name="pack",
    )(records)
    packed = pl.pallas_call(
        pick_kernel,
        out_shape=block_shape,
        in_specs=[vmem, vmem, vmem],
        out_specs=vmem,
        input_output_aliases={2: 0},
        compiler_params=pltpu.CompilerParams(vmem_limit_bytes=4 << 20),
        name="pick",
    )(sources.reshape(1, -1), records, packed)
    blocks = lax.all_to_all(packed, "chan", 0, 0, tiled=True)

    forward = jnp.asarray(front_tables(length, length // 32))
    inverse = jnp.asarray(inverse_tables(length, lag_count, factor))
    rows = 2 * LANES
    shape = jax.ShapeDtypeStruct
    turned = pl.pallas_call(
        level_kernel,
        out_shape=shape((rows, length), F32),
        in_specs=[vmem],
        out_specs=vmem,
        compiler_params=pltpu.CompilerParams(vmem_limit_bytes=16 << 20),
        cost_estimate=pl.CostEstimate(flops=1 << 28, bytes_accessed=1 << 20, transcendentals=0),
        name="level",
    )(blocks)
    white_re, white_im = pl.pallas_call(
        spectra_kernel,
        out_shape=(shape((rows, half), F32), shape((rows, half), F32)),
        in_specs=[vmem] * 2,
        out_specs=(vmem, vmem),
        compiler_params=pltpu.CompilerParams(vmem_limit_bytes=24 << 20),
        cost_estimate=pl.CostEstimate(flops=1 << 32, bytes_accessed=1 << 24, transcendentals=0),
        name="spectra",
    )(turned, forward)

    piece = shape((LANES, lag_count), F32)

    def stack(kind, after=None, handed=None):
        extra = [] if after is None else [after]
        outs = {
            "behind": [shape((2, LANES, lag_count), F32)],
            "ahead": [piece, piece],
        }.get(kind, [piece])
        rows = 2 * LANES if kind in ("behind", "ahead") else LANES
        scratch = [pltpu.VMEM((rows, length), BF16), pltpu.VMEM((rows, length), BF16)]
        if rows > LANES:
            scratch.append(pltpu.VMEM((2, LANES, lag_count), F32))
        aliases = {}
        if handed is not None:
            aliases = {3 + len(extra): 0}
            extra.append(handed)
            outs.insert(0, shape(handed.shape, F32))
        return pl.pallas_call(
            functools.partial(stack_kernel, kind),
            out_shape=outs,
            in_specs=[vmem] * (3 + len(extra)),
            out_specs=[vmem] * len(outs),
            scratch_shapes=scratch,
            input_output_aliases=aliases,
            compiler_params=pltpu.CompilerParams(vmem_limit_bytes=16 << 20),
            cost_estimate=pl.CostEstimate(flops=1 << 32, bytes_accessed=1 << 24, transcendentals=0),
            name="stack_" + kind,
        )(white_re, white_im, inverse, *extra)

    def small(kernel, outs, name, *operands):
        return pl.pallas_call(
            kernel,
            out_shape=[piece] * outs,
            in_specs=[vmem] * len(operands),
            out_specs=[vmem] * outs,
            compiler_params=pltpu.CompilerParams(vmem_limit_bytes=4 << 20),
            name=name,
        )(*operands)

    def onward(value):
        pairs = [(i, (i + (2 if i % 2 == 0 else -2)) % 8) for i in range(8)]
        return lax.ppermute(value, "win", pairs)

    def onward_other(value):
        pairs = [(i, (i + (3 if i % 2 == 0 else -3)) % 8) for i in range(8)]
        return lax.ppermute(value, "win", pairs)

    def across(value):
        return lax.ppermute(value, "win", [(i, i ^ 1) for i in range(8)])

    (send_far,) = stack("far_other")
    (keep_far,) = stack("far_own", after=send_far)
    (far,) = small(add_kernel, 1, "add_far", keep_far, across(send_far))
    passing = onward(far)
    (behind,) = stack("behind", after=far)
    own, other = stack("ahead", after=behind)
    own, other = small(join_kernel, 2, "join", own, other, across(behind))
    early = onward_other(other)
    (own,) = small(add_kernel, 1, "add_passing", own, passing)
    late = onward(own)
    (here_other,) = stack("here_other", after=other)
    (here_own,) = stack("here_own", after=here_other)
    result = (here_own + across(here_other)) + (early + late)
    return jnp.transpose(result.reshape(4, 32, lag_count), (0, 2, 1))


def solution(mesh):
    placed = (P("win", "chan", None), P())
    return jax.shard_map(
        local, mesh=mesh, in_specs=placed, out_specs=P("win", None, "chan"), check_vma=False
    )
```

```python
import functools
import math

import jax
import jax.numpy as jnp
import ml_dtypes
import numpy as np
from jax import lax
from jax.experimental import pallas as pl
from jax.experimental.pallas import tpu as pltpu
from jax.sharding import PartitionSpec as P

AMPLITUDE_FLOOR = 0.25
WHITE_EPSILON = 1e-06
HALF = 16
LANES = 128
F32 = jnp.float32
BF16 = jnp.bfloat16


def split_table(table):
    high = table.astype(np.float32).astype(ml_dtypes.bfloat16)
    low = (table - high.astype(np.float64)).astype(np.float32).astype(ml_dtypes.bfloat16)
    return high, low


def bin_order(half):
    return np.concatenate([np.arange(0, half, 4), np.arange(2, half, 4), np.arange(1, half, 2)])


def wave_table(length, bins, samples):
    angles = (np.arange(samples)[:, None] * bins[None, :] % length) * (2.0 * math.pi / length)
    return np.concatenate([np.cos(angles), -np.sin(angles)], axis=1)


def front_tables(length, reach):
    half = length // 2
    odd = wave_table(length, np.arange(1, half, 2), half)
    even = [wave_table(length, np.arange(start, half, 4), half // 2) for start in (0, 2)]
    bins = bin_order(half)
    band = (np.abs(bins[:, None] - bins[None, :]) <= reach).astype(ml_dtypes.bfloat16)
    waves = [*split_table(odd), *split_table(np.concatenate(even, axis=1))]
    return np.concatenate([*waves, band], axis=0)


def inverse_tables(length, lag_count, factor):
    half = length // 2
    bins = bin_order(half)
    lags = np.arange(lag_count) - lag_count // 2
    angles = (bins[:, None] * lags[None, :] % length) * (2.0 * math.pi / length)
    weights = np.where(bins == 0, 1.0, 2.0)[:, None] * factor
    return np.stack(
        split_table(np.concatenate([weights * np.cos(angles), -weights * np.sin(angles)], axis=1))
    )


def split(value):
    high = value.astype(BF16)
    return high, (value - high.astype(F32)).astype(BF16)


def mm(left, right):
    return jnp.dot(left, right, preferred_element_type=F32)


def pack_kernel(records, packed):
    windows, times, channels = records.shape
    dests = packed.shape[0]
    width = channels // dests
    per_tile = LANES // width
    lane = lax.broadcasted_iota(jnp.int32, (times, LANES), 1)
    for tile in range(channels // LANES):
        loaded = [records[w, :, tile * LANES : (tile + 1) * LANES] for w in range(windows)]
        for e in range(per_tile):
            block = None
            for w in range(windows):
                shift = (w - e) * width % LANES
                moved = pltpu.roll(loaded[w], shift, 1) if shift else loaded[w]
                block = moved if block is None else jnp.where(lane >= w * width, moved, block)
            packed[tile * per_tile + e, 0:times, :] = block


def pick_kernel(sources, records, packed_in, packed):
    windows, times, channels = records.shape
    dests = packed.shape[0]
    width = channels // dests
    per_tile = LANES // width
    lane = lax.broadcasted_iota(jnp.int32, (times, LANES), 1)
    place = jnp.concatenate([sources[...]] * windows, axis=1) & (LANES - 1)
    place = jnp.broadcast_to(place, (times, LANES))
    pick = jnp.zeros((times, LANES), F32)
    for tile in range(channels // LANES):
        for w in range(windows):
            loaded = records[w, :, tile * LANES : (tile + 1) * LANES]
            moved = jnp.take_along_axis(loaded, place, axis=1)
            low = w * dests + tile * per_tile
            pick = jnp.where((lane >= low) & (lane < low + per_tile), moved, pick)
    for d in range(dests):
        packed[d, times : 2 * times, :] = pick


def correlate(white_re, white_im, cross_high, cross_low, target, width, core=None):
    rows, half = white_re.shape
    lanes = rows // 2
    windows = lanes // width
    rows8 = [
        pl.ds(pl.multiple_of(lanes + w * width + target * 8, 8), 8) for w in range(windows)
    ]
    for tile in range(half // LANES):
        span = slice(tile * LANES, (tile + 1) * LANES)
        span2 = slice(half + tile * LANES, half + (tile + 1) * LANES)
        chan_re = [white_re[w * width : (w + 1) * width, span] for w in range(windows)]
        chan_im = [white_im[w * width : (w + 1) * width, span] for w in range(windows)]
        from_re = [white_re[at, span] for at in rows8]
        from_im = [white_im[at, span] for at in rows8]
        if core is not None:
            turn = lax.rem(8 - 4 * core, 8)
            from_re = [pltpu.roll(rows, turn, 0) for rows in from_re]
            from_im = [pltpu.roll(rows, turn, 0) for rows in from_im]
        chan_sum = [a + b for a, b in zip(chan_re, chan_im)]
        from_sum = [a + b for a, b in zip(from_re, from_im)]
        from_less = [a - b for a, b in zip(from_re, from_im)]
        for i in range(cross_high.shape[0] // width):
            for w in range(windows):
                one = jnp.broadcast_to(from_re[w][i : i + 1], (width, LANES)) * chan_sum[w]
                two = jnp.broadcast_to(from_less[w][i : i + 1], (width, LANES)) * chan_im[w]
                three = jnp.broadcast_to(from_sum[w][i : i + 1], (width, LANES)) * chan_re[w]
                ones = one if w == 0 else ones + one
                twos = two if w == 0 else twos + two
                threes = three if w == 0 else threes + three
            at = slice(i * width, (i + 1) * width)
            cross_high[at, span], cross_low[at, span] = split(ones - twos)
            cross_high[at, span2], cross_low[at, span2] = split(ones - threes)


def invert(cross_high, cross_low, tables):
    half = cross_high.shape[1] // 2
    lags = half // 2
    total = None
    for part in range(2):
        high = cross_high[:, part * half : (part + 1) * half]
        low = cross_low[:, part * half : (part + 1) * half]
        wave = tables[0, :, part * lags : (part + 1) * lags]
        rest = tables[1, :, part * lags : (part + 1) * lags]
        term = mm(high, wave) + mm(low, wave) + mm(high, rest)
        total = term if part == 0 else total + term
    return total


def level_kernel(blocks, turned):
    devices, double, lanes = blocks.shape
    times = double // 2
    length = devices * times
    for part in range(2):
        data = blocks[:, part * times : (part + 1) * times, :].reshape(length, lanes)
        level = jnp.abs(data)
        edge = jnp.zeros((HALF, lanes), F32)
        tail = jnp.concatenate([level, edge], axis=0)
        total = jnp.concatenate([edge, level, edge], axis=0)
        size = length + 2 * HALF
        for step in (1, 2, 4, 8, 16):
            total = total + pltpu.roll(total, size - step, 0)
        amplitude = (total[:length] + tail[HALF:]) * (1.0 / (2 * HALF + 1))
        normal = data / jnp.maximum(amplitude, AMPLITUDE_FLOOR)
        turned[part * lanes : (part + 1) * lanes, :] = normal.T


def spectra_kernel(turned, tables, white_re, white_im):
    length = turned.shape[1]
    half = length // 2
    quarter = half // 2
    eighth = quarter // 2

    def waves(row, rows, columns):
        return tables[row : row + rows, columns], tables[row + rows : row + 2 * rows, columns]

    def transform(data, table):
        high, low = split(data)
        return mm(high, table[0]) + mm(low, table[0]) + mm(high, table[1])

    first, second = turned[:, :half], turned[:, half:]
    odd = transform(first - second, waves(0, half, slice(0, half)))
    folded = first + second
    first, second = folded[:, :quarter], folded[:, quarter:]
    zero = transform(first + second, waves(length, quarter, slice(0, quarter)))
    two = transform(first - second, waves(length, quarter, slice(quarter, half)))
    re = jnp.concatenate([zero[:, :eighth], two[:, :eighth], odd[:, :quarter]], axis=1)
    im = jnp.concatenate([zero[:, eighth:], two[:, eighth:], odd[:, quarter:]], axis=1)
    high, low = split(jnp.sqrt(re * re + im * im))
    band = tables[length + half :, :]
    smooth = (mm(high, band) + mm(low, band)) * (1.0 / (2 * (length // 32) + 1))
    gain = 1.0 / (smooth + WHITE_EPSILON)
    white_re[...] = re * gain
    white_im[...] = im * gain


def stack_kernel(parts, white_re, white_im, tables, *refs):
    result, cross_high, cross_low = refs[-3:]
    win = lax.axis_index("win")
    z_hi, core = lax.div(win, 2), lax.rem(win, 2)
    for n, (step, own) in enumerate(parts):
        step = {"here": 0, "ahead": 1 + 2 * core, "far": 2, "behind": 3 - 2 * core}[step]
        target = lax.rem(z_hi + step, 4)
        high, low = cross_high.at[n], cross_low.at[n]
        correlate(white_re, white_im, high, low, target, 32, core if own else 1 - core)
        result[n] = invert(high, low, tables)


def add_kernel(*refs):
    total = refs[0][0]
    for ref in refs[1:-1]:
        total = total + (ref[0] if len(ref.shape) == 3 else ref[...])
    refs[-1][...] = total


def local(records, sources):
    chan_count = lax.axis_size("chan")
    windows, times, channels = records.shape
    length = times * chan_count
    lag_count = length // 4
    half = length // 2
    total_windows = windows * lax.axis_size("win")
    factor = 1.0 / math.sqrt(total_windows * half)
    vmem = pl.BlockSpec(memory_space=pltpu.VMEM)

    block_shape = jax.ShapeDtypeStruct((chan_count, 2 * times, LANES), F32)
    packed = pl.pallas_call(
        pack_kernel,
        out_shape=block_shape,
        in_specs=[vmem],
        out_specs=vmem,
        compiler_params=pltpu.CompilerParams(vmem_limit_bytes=4 << 20),
        cost_estimate=pl.CostEstimate(flops=1 << 31, bytes_accessed=1 << 20, transcendentals=0),
        name="pack",
    )(records)
    packed = pl.pallas_call(
        pick_kernel,
        out_shape=block_shape,
        in_specs=[vmem, vmem, vmem],
        out_specs=vmem,
        input_output_aliases={2: 0},
        compiler_params=pltpu.CompilerParams(vmem_limit_bytes=4 << 20),
        name="pick",
    )(sources.reshape(1, -1), records, packed)
    blocks = lax.all_to_all(packed, "chan", 0, 0, tiled=True)

    forward = jnp.asarray(front_tables(length, length // 32))
    inverse = jnp.asarray(inverse_tables(length, lag_count, factor))
    rows = 2 * LANES
    shape = jax.ShapeDtypeStruct
    turned = pl.pallas_call(
        level_kernel,
        out_shape=shape((rows, length), F32),
        in_specs=[vmem],
        out_specs=vmem,
        compiler_params=pltpu.CompilerParams(vmem_limit_bytes=16 << 20),
        cost_estimate=pl.CostEstimate(flops=1 << 28, bytes_accessed=1 << 20, transcendentals=0),
        name="level",
    )(blocks)
    white_re, white_im = pl.pallas_call(
        spectra_kernel,
        out_shape=(shape((rows, half), F32), shape((rows, half), F32)),
        in_specs=[vmem] * 2,
        out_specs=(vmem, vmem),
        compiler_params=pltpu.CompilerParams(vmem_limit_bytes=24 << 20),
        cost_estimate=pl.CostEstimate(flops=1 << 32, bytes_accessed=1 << 24, transcendentals=0),
        name="spectra",
    )(turned, forward)

    piece = shape((LANES, lag_count), F32)

    def stack(*parts, after=None):
        extra = [] if after is None else [after]
        count = len(parts)
        return pl.pallas_call(
            functools.partial(stack_kernel, parts),
            out_shape=shape((count, LANES, lag_count), F32),
            in_specs=[vmem] * (3 + len(extra)),
            out_specs=vmem,
            scratch_shapes=[pltpu.VMEM((count, LANES, length), BF16)] * 2,
            compiler_params=pltpu.CompilerParams(vmem_limit_bytes=16 << 20),
            cost_estimate=pl.CostEstimate(flops=count << 32, bytes_accessed=1, transcendentals=0),
            name="stack_" + "_".join(step for step, _ in parts),
        )(white_re, white_im, inverse, *extra)

    def add(name, *operands):
        return pl.pallas_call(
            add_kernel,
            out_shape=piece,
            in_specs=[vmem] * len(operands),
            out_specs=vmem,
            compiler_params=pltpu.CompilerParams(vmem_limit_bytes=4 << 20),
            name=name,
        )(*operands)

    def onward(value):
        pairs = [(i, (i + (2 if i % 2 == 0 else -2)) % 8) for i in range(8)]
        return lax.ppermute(value, "win", pairs)

    def onward_other(value):
        pairs = [(i, (i + (3 if i % 2 == 0 else -3)) % 8) for i in range(8)]
        return lax.ppermute(value, "win", pairs)

    def across(value):
        return lax.ppermute(value, "win", [(i, i ^ 1) for i in range(8)])

    far_other = stack(("far", False))
    far_own = stack(("far", True), after=far_other)
    far = add("add_far", far_own, across(far_other))
    passing = onward(far)
    behind_own = stack(("behind", True), after=far)
    ahead_other = stack(("ahead", False), after=behind_own)
    other = add("add_other", ahead_other, across(behind_own))
    early = onward_other(other)
    rest = stack(("behind", False), ("here", False), after=other)
    ahead_own = stack(("ahead", True), after=rest)
    rest = across(rest)
    own = add("add_own", ahead_own, rest, passing)
    late = onward(own)
    here_own = stack(("here", True), after=own)
    result = (here_own[0] + rest[1]) + (early + late)
    return jnp.transpose(result.reshape(4, 32, lag_count), (0, 2, 1))


def solution(mesh):
    placed = (P("win", "chan", None), P())
    return jax.shard_map(
        local, mesh=mesh, in_specs=placed, out_specs=P("win", None, "chan"), check_vma=False
    )
```

```python
import functools
import math

import jax
import jax.numpy as jnp
import ml_dtypes
import numpy as np
from jax import lax
from jax.experimental import pallas as pl
from jax.experimental.pallas import tpu as pltpu
from jax.sharding import PartitionSpec as P

AMPLITUDE_FLOOR = 0.25
WHITE_EPSILON = 1e-06
HALF = 16
LANES = 128
F32 = jnp.float32
BF16 = jnp.bfloat16


def split_table(table):
    high = table.astype(np.float32).astype(ml_dtypes.bfloat16)
    low = (table - high.astype(np.float64)).astype(np.float32).astype(ml_dtypes.bfloat16)
    return high, low


def bin_order(half):
    return np.concatenate([np.arange(0, half, 4), np.arange(2, half, 4), np.arange(1, half, 2)])


def wave_table(length, bins, samples):
    angles = (np.arange(samples)[:, None] * bins[None, :] % length) * (2.0 * math.pi / length)
    return np.concatenate([np.cos(angles), -np.sin(angles)], axis=1)


def front_tables(length, reach):
    half = length // 2
    odd = wave_table(length, np.arange(1, half, 2), half)
    even = [wave_table(length, np.arange(start, half, 4), half // 2) for start in (0, 2)]
    bins = bin_order(half)
    band = (np.abs(bins[:, None] - bins[None, :]) <= reach).astype(ml_dtypes.bfloat16)
    waves = [*split_table(odd), *split_table(np.concatenate(even, axis=1))]
    return np.concatenate([*waves, band], axis=0)


def inverse_tables(length, lag_count, factor):
    half = length // 2
    bins = bin_order(half)
    lags = np.arange(lag_count) - lag_count // 2
    angles = (bins[:, None] * lags[None, :] % length) * (2.0 * math.pi / length)
    weights = np.where(bins == 0, 1.0, 2.0)[:, None] * factor
    return np.stack(
        split_table(np.concatenate([weights * np.cos(angles), -weights * np.sin(angles)], axis=1))
    )


def split(value):
    high = value.astype(BF16)
    return high, (value - high.astype(F32)).astype(BF16)


def mm(left, right):
    return jnp.dot(left, right, preferred_element_type=F32)


def pack_kernel(records, packed):
    windows, times, channels = records.shape
    dests = packed.shape[0]
    width = channels // dests
    per_tile = LANES // width
    lane = lax.broadcasted_iota(jnp.int32, (times, LANES), 1)
    for tile in range(channels // LANES):
        loaded = [records[w, :, tile * LANES : (tile + 1) * LANES] for w in range(windows)]
        for e in range(per_tile):
            block = None
            for w in range(windows):
                shift = (w - e) * width % LANES
                moved = pltpu.roll(loaded[w], shift, 1) if shift else loaded[w]
                block = moved if block is None else jnp.where(lane >= w * width, moved, block)
            packed[tile * per_tile + e, 0:times, :] = block


def pick_kernel(sources, records, packed_in, packed):
    windows, times, channels = records.shape
    dests = packed.shape[0]
    width = channels // dests
    per_tile = LANES // width
    lane = lax.broadcasted_iota(jnp.int32, (times, LANES), 1)
    place = jnp.concatenate([sources[...]] * windows, axis=1) & (LANES - 1)
    place = jnp.broadcast_to(place, (times, LANES))
    pick = jnp.zeros((times, LANES), F32)
    for tile in range(channels // LANES):
        for w in range(windows):
            loaded = records[w, :, tile * LANES : (tile + 1) * LANES]
            moved = jnp.take_along_axis(loaded, place, axis=1)
            low = w * dests + tile * per_tile
            pick = jnp.where((lane >= low) & (lane < low + per_tile), moved, pick)
    for d in range(dests):
        packed[d, times : 2 * times, :] = pick


def correlate(white_re, white_im, cross_high, cross_low, target, width, core=None):
    rows, half = white_re.shape
    lanes = rows // 2
    windows = lanes // width
    rows8 = [
        pl.ds(pl.multiple_of(lanes + w * width + target * 8, 8), 8) for w in range(windows)
    ]
    for tile in range(half // LANES):
        span = slice(tile * LANES, (tile + 1) * LANES)
        span2 = slice(half + tile * LANES, half + (tile + 1) * LANES)
        chan_re = [white_re[w * width : (w + 1) * width, span] for w in range(windows)]
        chan_im = [white_im[w * width : (w + 1) * width, span] for w in range(windows)]
        from_re = [white_re[at, span] for at in rows8]
        from_im = [white_im[at, span] for at in rows8]
        if core is not None:
            turn = lax.rem(8 - 4 * core, 8)
            from_re = [pltpu.roll(rows, turn, 0) for rows in from_re]
            from_im = [pltpu.roll(rows, turn, 0) for rows in from_im]
        chan_sum = [a + b for a, b in zip(chan_re, chan_im)]
        from_sum = [a + b for a, b in zip(from_re, from_im)]
        from_less = [a - b for a, b in zip(from_re, from_im)]
        for i in range(cross_high.shape[0] // width):
            for w in range(windows):
                one = jnp.broadcast_to(from_re[w][i : i + 1], (width, LANES)) * chan_sum[w]
                two = jnp.broadcast_to(from_less[w][i : i + 1], (width, LANES)) * chan_im[w]
                three = jnp.broadcast_to(from_sum[w][i : i + 1], (width, LANES)) * chan_re[w]
                ones = one if w == 0 else ones + one
                twos = two if w == 0 else twos + two
                threes = three if w == 0 else threes + three
            at = slice(i * width, (i + 1) * width)
            cross_high[at, span], cross_low[at, span] = split(ones - twos)
            cross_high[at, span2], cross_low[at, span2] = split(ones - threes)


def invert(cross_high, cross_low, tables):
    half = cross_high.shape[1] // 2
    lags = half // 2
    total = None
    for part in range(2):
        high = cross_high[:, part * half : (part + 1) * half]
        low = cross_low[:, part * half : (part + 1) * half]
        wave = tables[0, :, part * lags : (part + 1) * lags]
        rest = tables[1, :, part * lags : (part + 1) * lags]
        term = mm(high, wave) + mm(low, wave) + mm(high, rest)
        total = term if part == 0 else total + term
    return total


def level_kernel(blocks, turned):
    devices, double, lanes = blocks.shape
    times = double // 2
    length = devices * times
    for part in range(2):
        data = blocks[:, part * times : (part + 1) * times, :].reshape(length, lanes)
        level = jnp.abs(data)
        edge = jnp.zeros((HALF, lanes), F32)
        tail = jnp.concatenate([level, edge], axis=0)
        total = jnp.concatenate([edge, level, edge], axis=0)
        size = length + 2 * HALF
        for step in (1, 2, 4, 8, 16):
            total = total + pltpu.roll(total, size - step, 0)
        amplitude = (total[:length] + tail[HALF:]) * (1.0 / (2 * HALF + 1))
        normal = data / jnp.maximum(amplitude, AMPLITUDE_FLOOR)
        turned[part * lanes : (part + 1) * lanes, :] = normal.T


def spectra_kernel(turned, tables, white_re, white_im):
    length = turned.shape[1]
    half = length // 2
    quarter = half // 2
    eighth = quarter // 2

    def waves(row, rows, columns):
        return tables[row : row + rows, columns], tables[row + rows : row + 2 * rows, columns]

    def transform(data, table):
        high, low = split(data)
        return mm(high, table[0]) + mm(low, table[0]) + mm(high, table[1])

    first, second = turned[:, :half], turned[:, half:]
    odd = transform(first - second, waves(0, half, slice(0, half)))
    folded = first + second
    first, second = folded[:, :quarter], folded[:, quarter:]
    zero = transform(first + second, waves(length, quarter, slice(0, quarter)))
    two = transform(first - second, waves(length, quarter, slice(quarter, half)))
    re = jnp.concatenate([zero[:, :eighth], two[:, :eighth], odd[:, :quarter]], axis=1)
    im = jnp.concatenate([zero[:, eighth:], two[:, eighth:], odd[:, quarter:]], axis=1)
    high, low = split(jnp.sqrt(re * re + im * im))
    band = tables[length + half :, :]
    smooth = (mm(high, band) + mm(low, band)) * (1.0 / (2 * (length // 32) + 1))
    gain = 1.0 / (smooth + WHITE_EPSILON)
    white_re[...] = re * gain
    white_im[...] = im * gain


def stack_kernel(parts, white_re, white_im, tables, *refs):
    result, cross_high, cross_low = refs[-3:]
    win = lax.axis_index("win")
    z_hi, core = lax.div(win, 2), lax.rem(win, 2)
    for n, (step, own) in enumerate(parts):
        step = {"here": 0, "ahead": 1 + 2 * core, "far": 2, "behind": 3 - 2 * core}[step]
        target = lax.rem(z_hi + step, 4)
        high, low = cross_high.at[n], cross_low.at[n]
        correlate(white_re, white_im, high, low, target, 32, core if own else 1 - core)
        result[n] = invert(high, low, tables)


def add_kernel(*refs):
    total = refs[0][0]
    for ref in refs[1:-1]:
        total = total + (ref[0] if len(ref.shape) == 3 else ref[...])
    refs[-1][...] = total


def add_far_kernel(own, other, total, token):
    total[...] = own[0] + other[0]
    token[...] = total[: token.shape[0], : token.shape[1]]


def local(records, sources):
    chan_count = lax.axis_size("chan")
    windows, times, channels = records.shape
    length = times * chan_count
    lag_count = length // 4
    half = length // 2
    total_windows = windows * lax.axis_size("win")
    factor = 1.0 / math.sqrt(total_windows * half)
    vmem = pl.BlockSpec(memory_space=pltpu.VMEM)

    block_shape = jax.ShapeDtypeStruct((chan_count, 2 * times, LANES), F32)
    packed = pl.pallas_call(
        pack_kernel,
        out_shape=block_shape,
        in_specs=[vmem],
        out_specs=vmem,
        compiler_params=pltpu.CompilerParams(vmem_limit_bytes=4 << 20),
        cost_estimate=pl.CostEstimate(flops=1 << 31, bytes_accessed=1 << 20, transcendentals=0),
        name="pack",
    )(records)
    packed = pl.pallas_call(
        pick_kernel,
        out_shape=block_shape,
        in_specs=[vmem, vmem, vmem],
        out_specs=vmem,
        input_output_aliases={2: 0},
        compiler_params=pltpu.CompilerParams(vmem_limit_bytes=4 << 20),
        name="pick",
    )(sources.reshape(1, -1), records, packed)
    blocks = lax.all_to_all(packed, "chan", 0, 0, tiled=True)

    forward = jnp.asarray(front_tables(length, length // 32))
    inverse = jnp.asarray(inverse_tables(length, lag_count, factor))
    rows = 2 * LANES
    shape = jax.ShapeDtypeStruct
    turned = pl.pallas_call(
        level_kernel,
        out_shape=shape((rows, length), F32),
        in_specs=[vmem],
        out_specs=vmem,
        compiler_params=pltpu.CompilerParams(vmem_limit_bytes=16 << 20),
        cost_estimate=pl.CostEstimate(flops=1 << 28, bytes_accessed=1 << 20, transcendentals=0),
        name="level",
    )(blocks)
    white_re, white_im = pl.pallas_call(
        spectra_kernel,
        out_shape=(shape((rows, half), F32), shape((rows, half), F32)),
        in_specs=[vmem] * 2,
        out_specs=(vmem, vmem),
        compiler_params=pltpu.CompilerParams(vmem_limit_bytes=24 << 20),
        cost_estimate=pl.CostEstimate(flops=1 << 32, bytes_accessed=1 << 24, transcendentals=0),
        name="spectra",
    )(turned, forward)

    piece = shape((LANES, lag_count), F32)

    def stack(*parts, after=None):
        extra = [] if after is None else [after]
        count = len(parts)
        return pl.pallas_call(
            functools.partial(stack_kernel, parts),
            out_shape=shape((count, LANES, lag_count), F32),
            in_specs=[vmem] * (3 + len(extra)),
            out_specs=vmem,
            scratch_shapes=[pltpu.VMEM((count, LANES, length), BF16)] * 2,
            compiler_params=pltpu.CompilerParams(vmem_limit_bytes=16 << 20),
            cost_estimate=pl.CostEstimate(flops=count << 32, bytes_accessed=1, transcendentals=0),
            name="stack_" + "_".join(step for step, _ in parts),
        )(white_re, white_im, inverse, *extra)

    def add(name, *operands):
        return pl.pallas_call(
            add_kernel,
            out_shape=piece,
            in_specs=[vmem] * len(operands),
            out_specs=vmem,
            compiler_params=pltpu.CompilerParams(vmem_limit_bytes=4 << 20),
            name=name,
        )(*operands)

    def onward(value):
        pairs = [(i, (i + (2 if i % 2 == 0 else -2)) % 8) for i in range(8)]
        return lax.ppermute(value, "win", pairs)

    def onward_other(value):
        pairs = [(i, (i + (3 if i % 2 == 0 else -3)) % 8) for i in range(8)]
        return lax.ppermute(value, "win", pairs)

    def across(value):
        return lax.ppermute(value, "win", [(i, i ^ 1) for i in range(8)])

    far_other = stack(("far", False))
    far_own = stack(("far", True), after=far_other)
    far, token = pl.pallas_call(
        add_far_kernel,
        out_shape=[piece, shape((8, LANES), F32)],
        in_specs=[vmem] * 2,
        out_specs=[vmem] * 2,
        compiler_params=pltpu.CompilerParams(vmem_limit_bytes=4 << 20),
        name="add_far",
    )(far_own, across(far_other))
    passing = onward(far)
    behind_own = stack(("behind", True), after=across(token))
    ahead_other = stack(("ahead", False), after=behind_own)
    other = add("add_other", ahead_other, across(behind_own))
    early = onward_other(other)
    rest = stack(("behind", False), ("here", False), after=other)
    ahead_own = stack(("ahead", True), after=rest)
    rest = across(rest)
    own = add("add_own", ahead_own, rest, passing)
    late = onward(own)
    here_own = stack(("here", True), after=own)
    result = (here_own[0] + rest[1]) + (early + late)
    return jnp.transpose(result.reshape(4, 32, lag_count), (0, 2, 1))


def solution(mesh):
    placed = (P("win", "chan", None), P())
    return jax.shard_map(
        local, mesh=mesh, in_specs=placed, out_specs=P("win", None, "chan"), check_vma=False
    )
```

```python
import functools
import math

import jax
import jax.numpy as jnp
import ml_dtypes
import numpy as np
from jax import lax
from jax.experimental import pallas as pl
from jax.experimental.pallas import tpu as pltpu
from jax.sharding import PartitionSpec as P

AMPLITUDE_FLOOR = 0.25
WHITE_EPSILON = 1e-06
HALF = 16
LANES = 128
F32 = jnp.float32
BF16 = jnp.bfloat16


def split_table(table):
    high = table.astype(np.float32).astype(ml_dtypes.bfloat16)
    low = (table - high.astype(np.float64)).astype(np.float32).astype(ml_dtypes.bfloat16)
    return high, low


def bin_order(half):
    return np.concatenate([np.arange(0, half, 4), np.arange(2, half, 4), np.arange(1, half, 2)])


def wave_table(length, bins, samples):
    angles = (np.arange(samples)[:, None] * bins[None, :] % length) * (2.0 * math.pi / length)
    return np.concatenate([np.cos(angles), -np.sin(angles)], axis=1)


def front_tables(length, reach):
    half = length // 2
    odd = wave_table(length, np.arange(1, half, 2), half)
    even = [wave_table(length, np.arange(start, half, 4), half // 2) for start in (0, 2)]
    bins = bin_order(half)
    band = (np.abs(bins[:, None] - bins[None, :]) <= reach).astype(ml_dtypes.bfloat16)
    waves = [*split_table(odd), *split_table(np.concatenate(even, axis=1))]
    return np.concatenate([*waves, band], axis=0)


def inverse_tables(length, lag_count, factor):
    half = length // 2
    bins = bin_order(half)
    lags = np.arange(lag_count) - lag_count // 2
    angles = (bins[:, None] * lags[None, :] % length) * (2.0 * math.pi / length)
    weights = np.where(bins == 0, 1.0, 2.0)[:, None] * factor
    return np.stack(
        split_table(np.concatenate([weights * np.cos(angles), -weights * np.sin(angles)], axis=1))
    )


def split(value):
    high = value.astype(BF16)
    return high, (value - high.astype(F32)).astype(BF16)


def mm(left, right):
    return jnp.dot(left, right, preferred_element_type=F32)


def pack_kernel(records, packed):
    windows, times, channels = records.shape
    dests = packed.shape[0]
    width = channels // dests
    per_tile = LANES // width
    lane = lax.broadcasted_iota(jnp.int32, (times, LANES), 1)
    for tile in range(channels // LANES):
        loaded = [records[w, :, tile * LANES : (tile + 1) * LANES] for w in range(windows)]
        for e in range(per_tile):
            block = None
            for w in range(windows):
                shift = (w - e) * width % LANES
                moved = pltpu.roll(loaded[w], shift, 1) if shift else loaded[w]
                block = moved if block is None else jnp.where(lane >= w * width, moved, block)
            packed[tile * per_tile + e, 0:times, :] = block


def pick_kernel(sources, records, packed_in, packed):
    windows, times, channels = records.shape
    dests = packed.shape[0]
    width = channels // dests
    per_tile = LANES // width
    lane = lax.broadcasted_iota(jnp.int32, (times, LANES), 1)
    place = jnp.concatenate([sources[...]] * windows, axis=1) & (LANES - 1)
    place = jnp.broadcast_to(place, (times, LANES))
    pick = jnp.zeros((times, LANES), F32)
    for tile in range(channels // LANES):
        for w in range(windows):
            loaded = records[w, :, tile * LANES : (tile + 1) * LANES]
            moved = jnp.take_along_axis(loaded, place, axis=1)
            low = w * dests + tile * per_tile
            pick = jnp.where((lane >= low) & (lane < low + per_tile), moved, pick)
    for d in range(dests):
        packed[d, times : 2 * times, :] = pick


def correlate(white_re, white_im, cross_high, cross_low, target, width, core=None):
    rows, half = white_re.shape
    lanes = rows // 2
    windows = lanes // width
    rows8 = [
        pl.ds(pl.multiple_of(lanes + w * width + target * 8, 8), 8) for w in range(windows)
    ]
    for tile in range(half // LANES):
        span = slice(tile * LANES, (tile + 1) * LANES)
        span2 = slice(half + tile * LANES, half + (tile + 1) * LANES)
        chan_re = [white_re[w * width : (w + 1) * width, span] for w in range(windows)]
        chan_im = [white_im[w * width : (w + 1) * width, span] for w in range(windows)]
        from_re = [white_re[at, span] for at in rows8]
        from_im = [white_im[at, span] for at in rows8]
        if core is not None:
            turn = lax.rem(8 - 4 * core, 8)
            from_re = [pltpu.roll(rows, turn, 0) for rows in from_re]
            from_im = [pltpu.roll(rows, turn, 0) for rows in from_im]
        chan_sum = [a + b for a, b in zip(chan_re, chan_im)]
        from_sum = [a + b for a, b in zip(from_re, from_im)]
        from_less = [a - b for a, b in zip(from_re, from_im)]
        for i in range(cross_high.shape[0] // width):
            for w in range(windows):
                one = jnp.broadcast_to(from_re[w][i : i + 1], (width, LANES)) * chan_sum[w]
                two = jnp.broadcast_to(from_less[w][i : i + 1], (width, LANES)) * chan_im[w]
                three = jnp.broadcast_to(from_sum[w][i : i + 1], (width, LANES)) * chan_re[w]
                ones = one if w == 0 else ones + one
                twos = two if w == 0 else twos + two
                threes = three if w == 0 else threes + three
            at = slice(i * width, (i + 1) * width)
            cross_high[at, span], cross_low[at, span] = split(ones - twos)
            cross_high[at, span2], cross_low[at, span2] = split(ones - threes)


def invert(cross_high, cross_low, tables):
    half = cross_high.shape[1] // 2
    lags = half // 2
    total = None
    for part in range(2):
        high = cross_high[:, part * half : (part + 1) * half]
        low = cross_low[:, part * half : (part + 1) * half]
        wave = tables[0, :, part * lags : (part + 1) * lags]
        rest = tables[1, :, part * lags : (part + 1) * lags]
        term = mm(high, wave) + mm(low, wave) + mm(high, rest)
        total = term if part == 0 else total + term
    return total


def level_kernel(blocks, turned):
    devices, double, lanes = blocks.shape
    times = double // 2
    length = devices * times
    for part in range(2):
        data = blocks[:, part * times : (part + 1) * times, :].reshape(length, lanes)
        level = jnp.abs(data)
        edge = jnp.zeros((HALF, lanes), F32)
        tail = jnp.concatenate([level, edge], axis=0)
        total = jnp.concatenate([edge, level, edge], axis=0)
        size = length + 2 * HALF
        for step in (1, 2, 4, 8, 16):
            total = total + pltpu.roll(total, size - step, 0)
        amplitude = (total[:length] + tail[HALF:]) * (1.0 / (2 * HALF + 1))
        normal = data / jnp.maximum(amplitude, AMPLITUDE_FLOOR)
        turned[part * lanes : (part + 1) * lanes, :] = normal.T


def spectra_kernel(turned, tables, white_re, white_im):
    length = turned.shape[1]
    half = length // 2
    quarter = half // 2
    eighth = quarter // 2

    def waves(row, rows, columns):
        return tables[row : row + rows, columns], tables[row + rows : row + 2 * rows, columns]

    def transform(data, table):
        high, low = split(data)
        return mm(high, table[0]) + mm(low, table[0]) + mm(high, table[1])

    first, second = turned[:, :half], turned[:, half:]
    odd = transform(first - second, waves(0, half, slice(0, half)))
    folded = first + second
    first, second = folded[:, :quarter], folded[:, quarter:]
    zero = transform(first + second, waves(length, quarter, slice(0, quarter)))
    two = transform(first - second, waves(length, quarter, slice(quarter, half)))
    re = jnp.concatenate([zero[:, :eighth], two[:, :eighth], odd[:, :quarter]], axis=1)
    im = jnp.concatenate([zero[:, eighth:], two[:, eighth:], odd[:, quarter:]], axis=1)
    high, low = split(jnp.sqrt(re * re + im * im))
    band = tables[length + half :, :]
    smooth = (mm(high, band) + mm(low, band)) * (1.0 / (2 * (length // 32) + 1))
    gain = 1.0 / (smooth + WHITE_EPSILON)
    white_re[...] = re * gain
    white_im[...] = im * gain


def stack_kernel(kind, white_re, white_im, tables, *refs):
    win = lax.axis_index("win")
    z_hi, core = lax.div(win, 2), lax.rem(win, 2)
    if kind.startswith(("far", "here")):
        result, cross_high, cross_low = refs[-3:]
        which = core if kind.endswith("own") else 1 - core
        target = lax.rem(z_hi + (2 if kind.startswith("far") else 0), 4)
        correlate(white_re, white_im, cross_high, cross_low, target, 32, which)
        result[...] = invert(cross_high, cross_low, tables)
        return
    cross_high, cross_low, both = refs[-3:]
    step = {"ahead": 1 + 2 * core, "behind": 3 - 2 * core}[kind]
    correlate(white_re, white_im, cross_high, cross_low, lax.rem(z_hi + step, 4), 32)
    both[...] = invert(cross_high, cross_low, tables).reshape(both.shape)
    if kind == "behind":
        refs[-4][0] = both[1 - core]
        refs[-4][1] = both[core]
    else:
        refs[-5][...] = both[core]
        refs[-4][...] = both[1 - core]


def add_kernel(*refs):
    half = len(refs) // 3
    for left, right, out in zip(refs[:half], refs[half : 2 * half], refs[2 * half :]):
        out[...] = left[...] + right[...]


def add_late_kernel(own, passing, total, token):
    total[...] = own[...] + passing[...]
    token[...] = total[: token.shape[0], : token.shape[1]]


def join_kernel(own, other, received, own_sum, other_sum):
    own_sum[...] = own[...] + received[0]
    other_sum[...] = other[...] + received[1]


def local(records, sources):
    chan_count = lax.axis_size("chan")
    windows, times, channels = records.shape
    length = times * chan_count
    lag_count = length // 4
    half = length // 2
    total_windows = windows * lax.axis_size("win")
    factor = 1.0 / math.sqrt(total_windows * half)
    vmem = pl.BlockSpec(memory_space=pltpu.VMEM)

    block_shape = jax.ShapeDtypeStruct((chan_count, 2 * times, LANES), F32)
    packed = pl.pallas_call(
        pack_kernel,
        out_shape=block_shape,
        in_specs=[vmem],
        out_specs=vmem,
        compiler_params=pltpu.CompilerParams(vmem_limit_bytes=4 << 20),
        cost_estimate=pl.CostEstimate(flops=1 << 31, bytes_accessed=1 << 20, transcendentals=0),
        name="pack",
    )(records)
    packed = pl.pallas_call(
        pick_kernel,
        out_shape=block_shape,
        in_specs=[vmem, vmem, vmem],
        out_specs=vmem,
        input_output_aliases={2: 0},
        compiler_params=pltpu.CompilerParams(vmem_limit_bytes=4 << 20),
        name="pick",
    )(sources.reshape(1, -1), records, packed)
    blocks = lax.all_to_all(packed, "chan", 0, 0, tiled=True)

    forward = jnp.asarray(front_tables(length, length // 32))
    inverse = jnp.asarray(inverse_tables(length, lag_count, factor))
    rows = 2 * LANES
    shape = jax.ShapeDtypeStruct
    turned = pl.pallas_call(
        level_kernel,
        out_shape=shape((rows, length), F32),
        in_specs=[vmem],
        out_specs=vmem,
        compiler_params=pltpu.CompilerParams(vmem_limit_bytes=16 << 20),
        cost_estimate=pl.CostEstimate(flops=1 << 28, bytes_accessed=1 << 20, transcendentals=0),
        name="level",
    )(blocks)
    white_re, white_im = pl.pallas_call(
        spectra_kernel,
        out_shape=(shape((rows, half), F32), shape((rows, half), F32)),
        in_specs=[vmem] * 2,
        out_specs=(vmem, vmem),
        compiler_params=pltpu.CompilerParams(vmem_limit_bytes=24 << 20),
        cost_estimate=pl.CostEstimate(flops=1 << 32, bytes_accessed=1 << 24, transcendentals=0),
        name="spectra",
    )(turned, forward)

    piece = shape((LANES, lag_count), F32)

    def stack(kind, after=None, handed=None):
        extra = [] if after is None else [after]
        outs = {
            "behind": [shape((2, LANES, lag_count), F32)],
            "ahead": [piece, piece],
        }.get(kind, [piece])
        rows = 2 * LANES if kind in ("behind", "ahead") else LANES
        scratch = [pltpu.VMEM((rows, length), BF16), pltpu.VMEM((rows, length), BF16)]
        if rows > LANES:
            scratch.append(pltpu.VMEM((2, LANES, lag_count), F32))
        aliases = {}
        if handed is not None:
            aliases = {3 + len(extra): 0}
            extra.append(handed)
            outs.insert(0, shape(handed.shape, F32))
        return pl.pallas_call(
            functools.partial(stack_kernel, kind),
            out_shape=outs,
            in_specs=[vmem] * (3 + len(extra)),
            out_specs=[vmem] * len(outs),
            scratch_shapes=scratch,
            input_output_aliases=aliases,
            compiler_params=pltpu.CompilerParams(vmem_limit_bytes=16 << 20),
            cost_estimate=pl.CostEstimate(flops=1 << 32, bytes_accessed=1 << 24, transcendentals=0),
            name="stack_" + kind,
        )(white_re, white_im, inverse, *extra)

    def small(kernel, outs, name, *operands):
        return pl.pallas_call(
            kernel,
            out_shape=[piece] * outs,
            in_specs=[vmem] * len(operands),
            out_specs=[vmem] * outs,
            compiler_params=pltpu.CompilerParams(vmem_limit_bytes=4 << 20),
            name=name,
        )(*operands)

    def onward(value):
        pairs = [(i, (i + (2 if i % 2 == 0 else -2)) % 8) for i in range(8)]
        return lax.ppermute(value, "win", pairs)

    def onward_other(value):
        pairs = [(i, (i + (3 if i % 2 == 0 else -3)) % 8) for i in range(8)]
        return lax.ppermute(value, "win", pairs)

    def across(value):
        return lax.ppermute(value, "win", [(i, i ^ 1) for i in range(8)])

    (send_far,) = stack("far_other")
    (keep_far,) = stack("far_own", after=send_far)
    (far,) = small(add_kernel, 1, "add_far", keep_far, across(send_far))
    passing = onward(far)
    (behind,) = stack("behind", after=far)
    own, other = stack("ahead", after=behind)
    own, other = small(join_kernel, 2, "join", own, other, across(behind))
    early = onward_other(other)
    own, token = pl.pallas_call(
        add_late_kernel,
        out_shape=[piece, shape((8, LANES), F32)],
        in_specs=[vmem] * 2,
        out_specs=[vmem] * 2,
        compiler_params=pltpu.CompilerParams(vmem_limit_bytes=4 << 20),
        name="add_passing",
    )(own, passing)
    late = onward(own)
    (here_other,) = stack("here_other", after=across(token))
    (here_own,) = stack("here_own", after=here_other)
    result = (here_own + across(here_other)) + (early + late)
    return jnp.transpose(result.reshape(4, 32, lag_count), (0, 2, 1))


def solution(mesh):
    placed = (P("win", "chan", None), P())
    return jax.shard_map(
        local, mesh=mesh, in_specs=placed, out_specs=P("win", None, "chan"), check_vma=False
    )
```

```python
import functools
import math

import jax
import jax.numpy as jnp
import ml_dtypes
import numpy as np
from jax import lax
from jax.experimental import pallas as pl
from jax.experimental.pallas import tpu as pltpu
from jax.sharding import PartitionSpec as P

AMPLITUDE_FLOOR = 0.25
WHITE_EPSILON = 1e-06
HALF = 16
LANES = 128
F32 = jnp.float32
BF16 = jnp.bfloat16


def split_table(table):
    high = table.astype(np.float32).astype(ml_dtypes.bfloat16)
    low = (table - high.astype(np.float64)).astype(np.float32).astype(ml_dtypes.bfloat16)
    return high, low


def bin_order(half):
    return np.concatenate([np.arange(0, half, 4), np.arange(2, half, 4), np.arange(1, half, 2)])


def wave_table(length, bins, samples):
    angles = (np.arange(samples)[:, None] * bins[None, :] % length) * (2.0 * math.pi / length)
    return np.concatenate([np.cos(angles), -np.sin(angles)], axis=1)


def front_tables(length, reach):
    half = length // 2
    odd = wave_table(length, np.arange(1, half, 2), half)
    even = [wave_table(length, np.arange(start, half, 4), half // 2) for start in (0, 2)]
    bins = bin_order(half)
    band = (np.abs(bins[:, None] - bins[None, :]) <= reach).astype(ml_dtypes.bfloat16)
    waves = [*split_table(odd), *split_table(np.concatenate(even, axis=1))]
    return np.concatenate([*waves, band], axis=0)


def inverse_tables(length, lag_count, factor):
    half = length // 2
    bins = bin_order(half)
    lags = np.arange(lag_count) - lag_count // 2
    angles = (bins[:, None] * lags[None, :] % length) * (2.0 * math.pi / length)
    weights = np.where(bins == 0, 1.0, 2.0)[:, None] * factor
    return np.stack(
        split_table(np.concatenate([weights * np.cos(angles), -weights * np.sin(angles)], axis=1))
    )


def split(value):
    high = value.astype(BF16)
    return high, (value - high.astype(F32)).astype(BF16)


def mm(left, right):
    return jnp.dot(left, right, preferred_element_type=F32)


def pack_kernel(records, packed):
    windows, times, channels = records.shape
    dests = packed.shape[0]
    width = channels // dests
    per_tile = LANES // width
    lane = lax.broadcasted_iota(jnp.int32, (times, LANES), 1)
    for tile in range(channels // LANES):
        loaded = [records[w, :, tile * LANES : (tile + 1) * LANES] for w in range(windows)]
        for e in range(per_tile):
            block = None
            for w in range(windows):
                shift = (w - e) * width % LANES
                moved = pltpu.roll(loaded[w], shift, 1) if shift else loaded[w]
                block = moved if block is None else jnp.where(lane >= w * width, moved, block)
            packed[tile * per_tile + e, 0:times, :] = block


def pick_kernel(sources, records, packed_in, packed):
    windows, times, channels = records.shape
    dests = packed.shape[0]
    width = channels // dests
    per_tile = LANES // width
    lane = lax.broadcasted_iota(jnp.int32, (times, LANES), 1)
    place = jnp.concatenate([sources[...]] * windows, axis=1) & (LANES - 1)
    place = jnp.broadcast_to(place, (times, LANES))
    pick = jnp.zeros((times, LANES), F32)
    for tile in range(channels // LANES):
        for w in range(windows):
            loaded = records[w, :, tile * LANES : (tile + 1) * LANES]
            moved = jnp.take_along_axis(loaded, place, axis=1)
            low = w * dests + tile * per_tile
            pick = jnp.where((lane >= low) & (lane < low + per_tile), moved, pick)
    for d in range(dests):
        packed[d, times : 2 * times, :] = pick


def correlate(white_re, white_im, cross_high, cross_low, target, width, core=None):
    rows, half = white_re.shape
    lanes = rows // 2
    windows = lanes // width
    rows8 = [
        pl.ds(pl.multiple_of(lanes + w * width + target * 8, 8), 8) for w in range(windows)
    ]
    for tile in range(half // LANES):
        span = slice(tile * LANES, (tile + 1) * LANES)
        span2 = slice(half + tile * LANES, half + (tile + 1) * LANES)
        chan_re = [white_re[w * width : (w + 1) * width, span] for w in range(windows)]
        chan_im = [white_im[w * width : (w + 1) * width, span] for w in range(windows)]
        from_re = [white_re[at, span] for at in rows8]
        from_im = [white_im[at, span] for at in rows8]
        if core is not None:
            turn = lax.rem(8 - 4 * core, 8)
            from_re = [pltpu.roll(rows, turn, 0) for rows in from_re]
            from_im = [pltpu.roll(rows, turn, 0) for rows in from_im]
        chan_sum = [a + b for a, b in zip(chan_re, chan_im)]
        from_sum = [a + b for a, b in zip(from_re, from_im)]
        from_less = [a - b for a, b in zip(from_re, from_im)]
        for i in range(cross_high.shape[0] // width):
            for w in range(windows):
                one = jnp.broadcast_to(from_re[w][i : i + 1], (width, LANES)) * chan_sum[w]
                two = jnp.broadcast_to(from_less[w][i : i + 1], (width, LANES)) * chan_im[w]
                three = jnp.broadcast_to(from_sum[w][i : i + 1], (width, LANES)) * chan_re[w]
                ones = one if w == 0 else ones + one
                twos = two if w == 0 else twos + two
                threes = three if w == 0 else threes + three
            at = slice(i * width, (i + 1) * width)
            cross_high[at, span], cross_low[at, span] = split(ones - twos)
            cross_high[at, span2], cross_low[at, span2] = split(ones - threes)


def invert(cross_high, cross_low, tables):
    half = cross_high.shape[1] // 2
    lags = half // 2
    total = None
    for part in range(2):
        high = cross_high[:, part * half : (part + 1) * half]
        low = cross_low[:, part * half : (part + 1) * half]
        wave = tables[0, :, part * lags : (part + 1) * lags]
        rest = tables[1, :, part * lags : (part + 1) * lags]
        term = mm(high, wave) + mm(low, wave) + mm(high, rest)
        total = term if part == 0 else total + term
    return total


def level_kernel(blocks, turned):
    devices, double, lanes = blocks.shape
    times = double // 2
    length = devices * times
    for part in range(2):
        data = blocks[:, part * times : (part + 1) * times, :].reshape(length, lanes)
        level = jnp.abs(data)
        edge = jnp.zeros((HALF, lanes), F32)
        tail = jnp.concatenate([level, edge], axis=0)
        total = jnp.concatenate([edge, level, edge], axis=0)
        size = length + 2 * HALF
        for step in (1, 2, 4, 8, 16):
            total = total + pltpu.roll(total, size - step, 0)
        amplitude = (total[:length] + tail[HALF:]) * (1.0 / (2 * HALF + 1))
        normal = data / jnp.maximum(amplitude, AMPLITUDE_FLOOR)
        turned[part * lanes : (part + 1) * lanes, :] = normal.T


def spectra_kernel(turned, tables, white_re, white_im):
    length = turned.shape[1]
    half = length // 2
    quarter = half // 2
    eighth = quarter // 2

    def waves(row, rows, columns):
        return tables[row : row + rows, columns], tables[row + rows : row + 2 * rows, columns]

    def transform(data, table):
        high, low = split(data)
        return mm(high, table[0]) + mm(low, table[0]) + mm(high, table[1])

    first, second = turned[:, :half], turned[:, half:]
    odd = transform(first - second, waves(0, half, slice(0, half)))
    folded = first + second
    first, second = folded[:, :quarter], folded[:, quarter:]
    zero = transform(first + second, waves(length, quarter, slice(0, quarter)))
    two = transform(first - second, waves(length, quarter, slice(quarter, half)))
    re = jnp.concatenate([zero[:, :eighth], two[:, :eighth], odd[:, :quarter]], axis=1)
    im = jnp.concatenate([zero[:, eighth:], two[:, eighth:], odd[:, quarter:]], axis=1)
    high, low = split(jnp.sqrt(re * re + im * im))
    band = tables[length + half :, :]
    smooth = (mm(high, band) + mm(low, band)) * (1.0 / (2 * (length // 32) + 1))
    gain = 1.0 / (smooth + WHITE_EPSILON)
    white_re[...] = re * gain
    white_im[...] = im * gain


def stack_kernel(parts, white_re, white_im, tables, *refs):
    result, cross_high, cross_low = refs[-3:]
    win = lax.axis_index("win")
    z_hi, core = lax.div(win, 2), lax.rem(win, 2)
    for n, (step, own) in enumerate(parts):
        step = {"here": 0, "ahead": 1 + 2 * core, "far": 2, "behind": 3 - 2 * core}[step]
        target = lax.rem(z_hi + step, 4)
        high, low = cross_high.at[n], cross_low.at[n]
        correlate(white_re, white_im, high, low, target, 32, core if own else 1 - core)
        result[n] = invert(high, low, tables)


def add_kernel(*refs):
    total = refs[0][0]
    for ref in refs[1:-1]:
        total = total + (ref[0] if len(ref.shape) == 3 else ref[...])
    refs[-1][...] = total


def local(records, sources):
    chan_count = lax.axis_size("chan")
    windows, times, channels = records.shape
    length = times * chan_count
    lag_count = length // 4
    half = length // 2
    total_windows = windows * lax.axis_size("win")
    factor = 1.0 / math.sqrt(total_windows * half)
    vmem = pl.BlockSpec(memory_space=pltpu.VMEM)

    block_shape = jax.ShapeDtypeStruct((chan_count, 2 * times, LANES), F32)
    packed = pl.pallas_call(
        pack_kernel,
        out_shape=block_shape,
        in_specs=[vmem],
        out_specs=vmem,
        compiler_params=pltpu.CompilerParams(vmem_limit_bytes=4 << 20),
        cost_estimate=pl.CostEstimate(flops=1 << 31, bytes_accessed=1 << 20, transcendentals=0),
        name="pack",
    )(records)
    packed = pl.pallas_call(
        pick_kernel,
        out_shape=block_shape,
        in_specs=[vmem, vmem, vmem],
        out_specs=vmem,
        input_output_aliases={2: 0},
        compiler_params=pltpu.CompilerParams(vmem_limit_bytes=4 << 20),
        name="pick",
    )(sources.reshape(1, -1), records, packed)
    blocks = lax.all_to_all(packed, "chan", 0, 0, tiled=True)

    forward = jnp.asarray(front_tables(length, length // 32))
    inverse = jnp.asarray(inverse_tables(length, lag_count, factor))
    rows = 2 * LANES
    shape = jax.ShapeDtypeStruct
    turned = pl.pallas_call(
        level_kernel,
        out_shape=shape((rows, length), F32),
        in_specs=[vmem],
        out_specs=vmem,
        compiler_params=pltpu.CompilerParams(vmem_limit_bytes=16 << 20),
        cost_estimate=pl.CostEstimate(flops=1 << 28, bytes_accessed=1 << 20, transcendentals=0),
        name="level",
    )(blocks)
    white_re, white_im = pl.pallas_call(
        spectra_kernel,
        out_shape=(shape((rows, half), F32), shape((rows, half), F32)),
        in_specs=[vmem] * 2,
        out_specs=(vmem, vmem),
        compiler_params=pltpu.CompilerParams(vmem_limit_bytes=24 << 20),
        cost_estimate=pl.CostEstimate(flops=1 << 32, bytes_accessed=1 << 24, transcendentals=0),
        name="spectra",
    )(turned, forward)

    piece = shape((LANES, lag_count), F32)

    def stack(*parts, after=None):
        extra = [] if after is None else [after]
        count = len(parts)
        return pl.pallas_call(
            functools.partial(stack_kernel, parts),
            out_shape=shape((count, LANES, lag_count), F32),
            in_specs=[vmem] * (3 + len(extra)),
            out_specs=vmem,
            scratch_shapes=[pltpu.VMEM((count, LANES, length), BF16)] * 2,
            compiler_params=pltpu.CompilerParams(vmem_limit_bytes=16 << 20),
            cost_estimate=pl.CostEstimate(flops=count << 32, bytes_accessed=1, transcendentals=0),
            name="stack_" + "_".join(step for step, _ in parts),
        )(white_re, white_im, inverse, *extra)

    def add(name, *operands):
        return pl.pallas_call(
            add_kernel,
            out_shape=piece,
            in_specs=[vmem] * len(operands),
            out_specs=vmem,
            compiler_params=pltpu.CompilerParams(vmem_limit_bytes=4 << 20),
            name=name,
        )(*operands)

    def onward(value):
        pairs = [(i, (i + (2 if i % 2 == 0 else -2)) % 8) for i in range(8)]
        return lax.ppermute(value, "win", pairs)

    def onward_other(value):
        pairs = [(i, (i + (3 if i % 2 == 0 else -3)) % 8) for i in range(8)]
        return lax.ppermute(value, "win", pairs)

    def across(value):
        return lax.ppermute(value, "win", [(i, i ^ 1) for i in range(8)])

    far_other = stack(("far", False))
    far_own = stack(("far", True), after=far_other)
    behind_own = stack(("behind", True), after=far_own)
    far = add("add_far", far_own, across(far_other))
    passing = onward(far)
    ahead_other = stack(("ahead", False), after=far)
    other = add("add_other", ahead_other, across(behind_own))
    early = onward_other(other)
    rest = stack(("behind", False), ("here", False), after=other)
    ahead_own = stack(("ahead", True), after=rest)
    rest = across(rest)
    own = add("add_own", ahead_own, rest, passing)
    late = onward(own)
    here_own = stack(("here", True), after=own)
    result = (here_own[0] + rest[1]) + (early + late)
    return jnp.transpose(result.reshape(4, 32, lag_count), (0, 2, 1))


def solution(mesh):
    placed = (P("win", "chan", None), P())
    return jax.shard_map(
        local, mesh=mesh, in_specs=placed, out_specs=P("win", None, "chan"), check_vma=False
    )
```
